512 devices in a mesh: grp: 64 (over y_lo, z, core), tp: 8 (over x, y_hi).
Axes of the slice: x: 4, y: 4 (y_hi: 2, y_lo: 2; y = y_hi * 2 + y_lo), z: 16, core: 2. Of those that a mesh axis runs over, the one named last changes fastest.
Arguments:
- queries: bfloat16 [64, 2, 512, 2048], P('grp', None, None, 'tp'), may hold values from -9 to 9
- fresh_kv: bfloat16 [64, 2, 512, 2, 2048], P('grp', None, None, None, 'tp'), may hold values from -9 to 9
- stale_kv: bfloat16 [64, 2, 512, 2, 2048], P('grp', None, None, None, 'tp'), may hold values from -6 to 6
- text_kv: bfloat16 [64, 2, 256, 2, 2048], P('grp', None, None, None, 'tp'), may hold values from -6 to 6
- w_velocity: bfloat16 [2048, 64], P('tp'), may hold values from -2.390625 to 2.390625
- latent: float32 [64, 2, 512, 64], P('grp', None, 'tp'), may hold values from -6 to 6
- live_counts: int32 [64, 2], replicated, may hold values from 128 to 512, as said below
- refresh_rows: int32 [64, 2, 64], replicated, may hold values from 0 to 511, as said below
- request_list: int32 [64], replicated, may hold values from 0 to 63, each once
- timesteps: int32 [64, 2], replicated, may hold values from 0 to 999, as said below
Outputs:
- next_stale: bfloat16 [64, 2, 512, 2, 2048], P('grp', None, None, None, 'tp')
- velocity: float32 [64, 2, 512, 64], P('grp', None, 'tp')
- latent_next: float32 [64, 2, 512, 64], P('grp', None, 'tp')
The draws below stay inside these ranges and needn't reach their ends.
Inputs may be any that keep to these rules, and one draw needn't show every extreme that they name: `live_counts`: 512 is reached in every draw. `refresh_rows`: rows within one list are distinct. `timesteps`: the next timestep is below the current one. `request_list`: each request appears once.
All inputs are finite; a program needn't handle non-finite values.
Results may differ from the reference program's by a relative error of at most 0.0045.
Values may be sent and summed in bfloat16 or wider, within the bound.
A program may use at most 64 MiB of HBM per device.

```python
import math
import jax
import jax.numpy as jnp
from jax import lax

HEADS = 16
HD = 128
INNER = 2048
CH = 64
IMG_DEV = 512
TXT_DEV = 256
REQ_DEV = 2
RECOMP = 64
GROUPS = 64
REQUESTS = 64
N_GRP = 64


def draw_queries(key, part):
    shape = (GROUPS, REQ_DEV, IMG_DEV, HEADS * HD)
    base = 1.2 * jnp.clip(jax.random.normal(jax.random.fold_in(key, 1), shape, jnp.float32), -6.0, 6.0)
    return base.astype(jnp.bfloat16)


def draw_fresh_kv(key, part):
    shape = (GROUPS, REQ_DEV, IMG_DEV, 2, HEADS * HD)
    base = jnp.clip(jax.random.normal(jax.random.fold_in(key, 2), shape, jnp.float32), -6.0, 6.0)
    return base.astype(jnp.bfloat16)


def draw_live_counts(key, part):
    counts = jax.random.randint(jax.random.fold_in(key, 3), (GROUPS * REQ_DEV,), IMG_DEV // 4, IMG_DEV + 1)
    chosen = jax.random.randint(jax.random.fold_in(key, 4), (), 0, GROUPS * REQ_DEV)
    counts = jnp.where(jnp.arange(GROUPS * REQ_DEV) == chosen, IMG_DEV, counts)
    return counts.reshape(GROUPS, REQ_DEV).astype(jnp.int32)


def draw_refresh_rows(key, part):
    streams = jax.random.split(jax.random.fold_in(key, 5), GROUPS * REQ_DEV)
    row_lists = jax.vmap(lambda stream: jax.random.permutation(stream, IMG_DEV)[:RECOMP])(streams)
    return row_lists.reshape(GROUPS, REQ_DEV, RECOMP).astype(jnp.int32)


def draw_timesteps(key, part):
    starts = jax.random.randint(jax.random.fold_in(key, 6), (REQUESTS,), 400, 1000)
    strides = jax.random.randint(jax.random.fold_in(key, 8), (REQUESTS,), 100, 400)
    return jnp.stack([starts, starts - strides], axis=1).astype(jnp.int32)


def block_scale(rng, extent, cuts, smallest, top_value):
    def one(position, blocks):
        draws = jax.random.uniform(jax.random.fold_in(jax.random.fold_in(rng, 6), position), (blocks,), jnp.float32, smallest / len(cuts), top_value / len(cuts))
        return jnp.repeat(jnp.exp(draws), extent[position] // blocks).reshape((-1,) + (1,) * (len(extent) - position - 1))

    level = one(*cuts[0])
    for cut in cuts[1:]:
        level = level * one(*cut)
    return level


def gaussian(stream_key, extent, spread, limit, pieces=(), kind=jnp.bfloat16):
    drawn = spread * jax.random.normal(stream_key, extent, jnp.float32)
    if pieces:
        drawn = drawn * block_scale(stream_key, extent, pieces, -0.22, 0.18)
    return jnp.clip(drawn, -limit, limit).astype(kind)


def setup_inputs(seed: int = 0) -> dict:
    key_of = jax.random.split(jax.random.key(seed), 11)
    queries = draw_queries(jax.random.fold_in(key_of[10], 71), 0)
    fresh_kv = draw_fresh_kv(jax.random.fold_in(key_of[10], 71), 0)
    stale_kv = gaussian(key_of[2], (GROUPS, REQ_DEV, IMG_DEV, 2, INNER), 1.0, 6.0, ((0, 64), (4, 8)))
    text_kv = gaussian(key_of[3], (GROUPS, REQ_DEV, TXT_DEV, 2, INNER), 1.0, 6.0, ((0, 64), (4, 8)))
    w_velocity = gaussian(key_of[4], (INNER, CH), 0.4, 2.390625, ((0, 8),))
    latent = gaussian(key_of[5], (GROUPS, REQ_DEV, IMG_DEV, CH), 1.0, 6.0, ((0, 64), (2, 8)), jnp.float32)
    live_counts = draw_live_counts(jax.random.fold_in(key_of[10], 71), 0)
    refresh_rows = draw_refresh_rows(jax.random.fold_in(key_of[10], 71), 0)
    request_list = jax.random.permutation(key_of[8], REQUESTS).astype(jnp.int32)
    timesteps = draw_timesteps(jax.random.fold_in(key_of[10], 71), 0)
    return dict(queries=queries, fresh_kv=fresh_kv, stale_kv=stale_kv, text_kv=text_kv, w_velocity=w_velocity, latent=latent, live_counts=live_counts, refresh_rows=refresh_rows, request_list=request_list, timesteps=timesteps)


def slot_velocity(slot_query, own_kv, partner_kv, text_pair, own_live, partner_live, w_velocity):
    key_rows = jnp.concatenate([own_kv[:, 0], partner_kv[:, 0], text_pair[:, 0]], axis=0)
    value_rows = jnp.concatenate([own_kv[:, 1], partner_kv[:, 1], text_pair[:, 1]], axis=0)
    row_ids = jnp.arange(IMG_DEV, dtype=jnp.int32)
    live_mask = jnp.concatenate([row_ids < own_live, row_ids < partner_live, jnp.ones((2 * TXT_DEV,), dtype=bool)])
    query_float = slot_query.astype(jnp.float32).reshape(IMG_DEV, HEADS, HD)
    key_float = key_rows.astype(jnp.float32).reshape(-1, HEADS, HD)
    value_float = value_rows.astype(jnp.float32).reshape(-1, HEADS, HD)
    scores = jnp.einsum('qhd,khd->hqk', query_float, key_float) * (1.0 / math.sqrt(HD))
    scores = jnp.where(live_mask[None, None, :], scores, -jnp.inf)
    row_top = lax.optimization_barrier(jnp.max(scores, axis=2, keepdims=True))
    weights = jnp.exp(scores - row_top)
    totals = lax.optimization_barrier(jnp.sum(weights, axis=2))
    rounded = weights.astype(jnp.bfloat16).astype(jnp.float32)
    blended = jnp.einsum('hqk,khd->qhd', rounded, value_float) / jnp.transpose(totals)[:, :, None]
    blended = blended.reshape(IMG_DEV, HEADS * HD).astype(jnp.bfloat16)
    velocity = jnp.dot(blended, w_velocity, preferred_element_type=jnp.float32)
    return jnp.where((row_ids < own_live)[:, None], velocity, 0.0)

def reference(queries, fresh_kv, stale_kv, text_kv, w_velocity, latent, live_counts, refresh_rows, request_list, timesteps):
    half_groups = N_GRP // 2

    def per_group(group_index):
        partner = (group_index + half_groups) % N_GRP
        partner_fresh = fresh_kv[partner]
        velocities = []
        latents = []
        for slot_index in range(REQ_DEV):
            listed = refresh_rows[partner, slot_index].astype(jnp.int32)
            repaired = stale_kv[group_index, slot_index].at[listed].set(partner_fresh[slot_index][listed])
            text_pair = jnp.concatenate([text_kv[group_index, slot_index], text_kv[partner, slot_index]], axis=0)
            velocity = slot_velocity(queries[group_index, slot_index], fresh_kv[group_index, slot_index], repaired, text_pair, live_counts[group_index, slot_index], live_counts[partner, slot_index], w_velocity)
            request_id = request_list[group_index % half_groups * REQ_DEV + slot_index]
            times = timesteps[request_id]
            step_size = (times[1] - times[0]).astype(jnp.float32) / 1000.0
            velocities.append(velocity)
            latents.append(latent[group_index, slot_index] + step_size * velocity)
        return (jnp.stack(velocities), jnp.stack(latents))
    velocity, latent_next = lax.map(per_group, jnp.arange(N_GRP, dtype=jnp.int32))
    next_stale = jnp.roll(fresh_kv, half_groups, axis=0)
    return (next_stale, velocity, latent_next)
```

```python
import math

import jax
import jax.numpy as jnp
from jax import lax
from jax.experimental.layout import Layout, with_layout_constraint
from jax.experimental import pallas as pl
from jax.experimental.pallas import tpu as pltpu
from jax.sharding import PartitionSpec as P

HD = 128
TILE = 128
SCALE = math.log2(math.e) / math.sqrt(HD)
VMEM = pltpu.MemorySpace.VMEM
SMEM = pltpu.MemorySpace.SMEM


def whole(space):
    return pl.BlockSpec(memory_space=space)


def from_behind(block, axis, distance):
    devices = range(lax.axis_size(axis))
    route = [((i - distance) % len(devices), i) for i in devices]
    return lax.ppermute(block, axis, route)


def swap_rows(lists, group, sub, flag, free, rows, listed):
    keep = rows - listed
    slots = sub.shape[0]
    step = 8

    def over(body, first):
        return lax.fori_loop(0, listed // step, body, first)

    def ids(i):
        return [(s, i * step + k) for k in range(step) for s in range(slots)]

    def clear(i, carry):
        for s, j in ids(i):
            flag[s, j] = 0
        return carry

    over(clear, 0)

    def mark(i, carry):
        found = [(s, lists[group, s, j]) for s, j in ids(i)]
        for s, row in found:
            flag[s, jnp.where(row >= keep, row - keep, listed)] = 1
        return carry

    over(mark, 0)

    def collect(i, counts):
        counts = list(counts)
        taken = [(s, j, flag[s, j]) for s, j in ids(i)]
        for s, j, used in taken:
            free[s, counts[s]] = j + keep
            counts[s] = counts[s] + (1 - used)
        return tuple(counts)

    over(collect, (0,) * slots)

    def assign(i, counts):
        counts = list(counts)
        found = [(s, j, lists[group, s, j]) for s, j in ids(i)]
        result = []
        for s, j, row in found:
            low = row < keep
            result.append((s, j, jnp.where(low, free[s, counts[s]], row)))
            counts[s] = counts[s] + low.astype(jnp.int32)
        for s, j, row in result:
            sub[s, j] = row
        return tuple(counts)

    over(assign, (0,) * slots)


def pack_kernel(lists, fresh, early, bulk, held, sub, flag, free, in_sem, out_sem):
    _, slots, rows, _, _ = fresh.shape
    listed = early.shape[2]
    keep = rows - listed
    group = lax.axis_index("grp")
    loads = [
        pltpu.make_async_copy(fresh.at[0, s], held.at[s], in_sem.at[s])
        for s in range(slots)
    ]
    for load in loads:
        load.start()
    stores = []
    swap_rows(lists, group, sub, flag, free, rows, listed)
    step = 8
    for s in range(slots):
        loads[s].wait()

        def exchange(i, carry, s=s):
            ids = [i * step + k for k in range(step)]
            at = [lists[group, s, j] for j in ids]
            to = [sub[s, j] for j in ids]
            taken = [held[s, row] for row in at]
            given = [held[s, row] for row in to]
            for k in range(step):
                early[0, s, ids[k]] = taken[k]
            for k in range(step):
                held[s, at[k]] = given[k]
            return carry

        lax.fori_loop(0, listed // step, exchange, 0)
        store = pltpu.make_async_copy(
            held.at[s, pl.ds(0, keep)], bulk.at[0, s], out_sem.at[s]
        )
        store.start()
        stores.append(store)
    for store in stores:
        store.wait()


def pack(refresh_rows, fresh_kv):
    _, slots, rows, two, width = fresh_kv.shape
    listed = refresh_rows.shape[2]
    keep = rows - listed
    kv = fresh_kv.dtype
    return pl.pallas_call(
        pack_kernel,
        out_shape=(
            jax.ShapeDtypeStruct((1, slots, listed, two, width), kv),
            jax.ShapeDtypeStruct((1, slots, keep, two, width), kv),
        ),
        in_specs=[whole(SMEM), whole(pl.ANY)],
        out_specs=(whole(VMEM), whole(pl.ANY)),
        scratch_shapes=[
            pltpu.VMEM((slots, rows, two, width), kv),
            pltpu.SMEM((slots, listed), jnp.int32),
            pltpu.SMEM((slots, listed + 1), jnp.int32),
            pltpu.SMEM((slots, listed + 1), jnp.int32),
            pltpu.SemaphoreType.DMA((slots,)),
            pltpu.SemaphoreType.DMA((slots,)),
        ],
        compiler_params=pltpu.CompilerParams(vmem_limit_bytes=8 << 20),
        cost_estimate=pl.CostEstimate(
            flops=0, transcendentals=0, bytes_accessed=4 << 20
        ),
        name="pack",
    )(refresh_rows, fresh_kv)


def place_rows(lists, group, sub, early, held, slot):
    step = 8

    def place(i, carry):
        ids = [i * step + k for k in range(step)]
        at = [lists[group, slot, j] for j in ids]
        to = [sub[slot, j] for j in ids]
        moved = [held[slot, row] for row in at]
        new = [early[0, slot, j] for j in ids]
        for k in range(step):
            held[slot, to[k]] = moved[k]
        for k in range(step):
            held[slot, at[k]] = new[k]
        return carry

    lax.fori_loop(0, early.shape[2] // step, place, 0)


def unpack_kernel(lists, sub, early, bulk, after, out, held, in_sem, out_sem):
    _, slots, rows, _, _ = out.shape
    keep = rows - early.shape[2]
    partner = lax.rem(
        lax.axis_index("grp") + lax.axis_size("grp") // 2, lax.axis_size("grp")
    )
    loads = [
        pltpu.make_async_copy(
            bulk.at[0, s], held.at[s, pl.ds(0, keep)], in_sem.at[s]
        )
        for s in range(slots)
    ]
    for load in loads:
        load.start()
    stores = []
    for s in range(slots):
        loads[s].wait()
        place_rows(lists, partner, sub, early, held, s)
        store = pltpu.make_async_copy(held.at[s], out.at[0, s], out_sem.at[s])
        store.start()
        stores.append(store)
    for store in stores:
        store.wait()


def unpack(refresh_rows, sub, early, bulk, after):
    _, slots, listed, two, width = early.shape
    rows = bulk.shape[2] + listed
    kv = bulk.dtype
    return pl.pallas_call(
        unpack_kernel,
        out_shape=jax.ShapeDtypeStruct((1, slots, rows, two, width), kv),
        in_specs=[
            whole(SMEM),
            whole(SMEM),
            whole(VMEM),
            whole(pl.ANY),
            whole(pl.ANY),
        ],
        out_specs=whole(pl.ANY),
        scratch_shapes=[
            pltpu.VMEM((slots, rows, two, width), kv),
            pltpu.SemaphoreType.DMA((slots,)),
            pltpu.SemaphoreType.DMA((slots,)),
        ],
        compiler_params=pltpu.CompilerParams(vmem_limit_bytes=8 << 20),
        cost_estimate=pl.CostEstimate(
            flops=0, transcendentals=0, bytes_accessed=4 << 20
        ),
        name="unpack",
    )(refresh_rows, sub, early, bulk, after)


def prepare_kernel(lists, live, bias, sub, flag, free):
    slots = bias.shape[0]
    listed = lists.shape[2]
    rows = (bias.shape[2] - TILE) // 2
    groups = lax.axis_size("grp")
    group = lax.axis_index("grp")
    partner = lax.rem(group + groups // 2, groups)
    ids = lax.broadcasted_iota(jnp.int32, (1, rows), 1)
    early_ids = lax.broadcasted_iota(jnp.int32, (1, TILE), 1)
    dead = jnp.float32(-jnp.inf)
    for s in range(slots):
        partner_live = live[s, partner]

        def mark(j, carry, s=s):
            stale_bias, early_row = carry
            row = lists[partner, s, j]
            stale_bias = jnp.where(ids == row, dead, stale_bias)
            early_row = jnp.where(early_ids == j, row, early_row)
            return stale_bias, early_row

        stale_bias, early_row = lax.fori_loop(
            0,
            listed,
            mark,
            (
                jnp.where(ids < partner_live, 0.0, dead),
                jnp.full((1, TILE), rows, jnp.int32),
            ),
            unroll=8,
        )
        bias[s, :, :rows] = jnp.where(ids < live[s, group], 0.0, dead)
        bias[s, :, rows : 2 * rows] = stale_bias
        bias[s, :, 2 * rows :] = jnp.where(early_row < partner_live, 0.0, dead)
    swap_rows(lists, partner, sub, flag, free, rows, listed)


def prepare(refresh_rows, live_t, rows):
    _, slots, listed = refresh_rows.shape
    return pl.pallas_call(
        prepare_kernel,
        out_shape=(
            jax.ShapeDtypeStruct((slots, 1, 2 * rows + TILE), jnp.float32),
            jax.ShapeDtypeStruct((slots, listed), jnp.int32),
        ),
        in_specs=[whole(SMEM), whole(SMEM)],
        out_specs=(whole(VMEM), whole(SMEM)),
        scratch_shapes=[
            pltpu.SMEM((slots, listed + 1), jnp.int32),
            pltpu.SMEM((slots, listed + 1), jnp.int32),
        ],
        compiler_params=pltpu.CompilerParams(vmem_limit_bytes=4 << 20),
        cost_estimate=pl.CostEstimate(
            flops=0, transcendentals=0, bytes_accessed=1 << 20
        ),
        name="prepare",
    )(refresh_rows, live_t)


def tiles(array):
    return [array[:, i : i + TILE] for i in range(0, array.shape[1], TILE)]


def attend_kernel(
    bias, q, own, stale, text, text_other, early, w_t, out, scores, acc
):
    slot, head = pl.program_id(0), pl.program_id(1)
    rows = own.shape[2]
    query = q[0, 0]
    blocks = (
        (own, bias[0, :, :rows]),
        (stale, bias[0, :, rows : 2 * rows]),
        (early, bias[0, :, 2 * rows :]),
        (text, None),
        (text_other, None),
    )
    top = None
    first = 0
    spans = []
    for block, block_bias in blocks:
        s = lax.dot_general(
            query,
            block[0, 0],
            (((1,), (1,)), ((), ())),
            preferred_element_type=jnp.float32,
        )
        if block_bias is not None:
            s = s + block_bias
        count = s.shape[1]
        scores[:, first : first + count] = s
        spans.append((first, count))
        first += count
        for tile in tiles(s):
            top = tile if top is None else jnp.maximum(top, tile)
    shift = jnp.max(top, axis=1, keepdims=True) * SCALE
    totals = None
    blended = None
    for (block, _), (first, count) in zip(blocks, spans):
        weights = jnp.exp2(scores[:, first : first + count] * SCALE - shift)
        for tile in tiles(weights):
            totals = tile if totals is None else totals + tile
        part = jnp.dot(
            weights.astype(jnp.bfloat16),
            block[0, 1],
            preferred_element_type=jnp.float32,
        )
        blended = part if blended is None else blended + part
    totals = jnp.sum(totals, axis=1, keepdims=True)
    blended = (blended / totals).astype(jnp.bfloat16)
    v = lax.dot_general(
        blended,
        w_t[...],
        (((1,), (1,)), ((), ())),
        preferred_element_type=jnp.float32,
    )

    @pl.when(head == 0)
    def _():
        acc[...] = v

    @pl.when(head > 0)
    def _():
        acc[...] += v

    width = v.shape[1]
    last = head == pl.num_programs(1) - 1

    for s in range(2):

        @pl.when(jnp.logical_and(last, slot == s))
        def _(s=s):
            out[:, s * width : (s + 1) * width] = acc[...]


def attend(bias, queries, own, stale, text, text_other, early, w_t):
    _, slots, rows, inner = queries.shape
    heads = inner // HD
    ch = w_t.shape[0]
    keys = sum(a.shape[2] for a in (own, stale, text, text_other, early))

    def kv_spec(a):
        return pl.BlockSpec((1, 2, a.shape[2], HD), lambda s, h: (s, 0, 0, h))

    return pl.pallas_call(
        attend_kernel,
        grid=(slots, heads),
        out_shape=jax.ShapeDtypeStruct((rows, slots * ch), jnp.float32),
        in_specs=[
            pl.BlockSpec((1, 1, bias.shape[2]), lambda s, h: (s, 0, 0)),
            pl.BlockSpec((1, 1, rows, HD), lambda s, h: (0, s, 0, h)),
            kv_spec(own),
            kv_spec(stale),
            kv_spec(text),
            kv_spec(text_other),
            kv_spec(early),
            pl.BlockSpec((ch, HD), lambda s, h: (0, h)),
        ],
        out_specs=pl.BlockSpec((rows, slots * ch), lambda s, h: (0, 0)),
        scratch_shapes=[
            pltpu.VMEM((rows, keys), jnp.float32),
            pltpu.VMEM((rows, ch), jnp.float32),
        ],
        compiler_params=pltpu.CompilerParams(vmem_limit_bytes=24 << 20),
        cost_estimate=pl.CostEstimate(
            flops=20 * slots * heads * rows * keys * HD,
            transcendentals=slots * heads * rows * keys,
            bytes_accessed=4 << 20,
        ),
        name="attend",
    )(bias, queries, own, stale, text, text_other, early, w_t)


def tp_sum_kernel(
    part, out, leaving, arrived, mine, crossing, other, send, recv, send2, recv2
):
    t = lax.axis_index("tp")
    x, half = t // 2, lax.rem(t, 2)
    sides = lax.axis_size("tp") // 2
    share = out.shape[0]
    pair = 2 * share
    peers = [lax.rem(x + d, sides) for d in range(1, sides)]
    across = x * 2 + 1 - half

    barrier = pltpu.get_barrier_semaphore()
    for peer in peers:
        pl.semaphore_signal(
            barrier,
            inc=1,
            device_id={"tp": peer * 2 + half},
            device_id_type=pl.DeviceIdType.MESH,
        )
    pl.semaphore_signal(
        barrier,
        inc=1,
        device_id={"tp": across},
        device_id_type=pl.DeviceIdType.MESH,
    )
    leaving[...] = part[...].astype(leaving.dtype)
    pl.semaphore_wait(barrier, sides)

    copies = []
    for i, peer in enumerate(peers):
        copy = pltpu.make_async_remote_copy(
            src_ref=leaving.at[pl.ds(pl.multiple_of(peer * pair, 16), pair)],
            dst_ref=arrived.at[i],
            send_sem=send.at[i],
            recv_sem=recv.at[i],
            device_id={"tp": peer * 2 + half},
            device_id_type=pl.DeviceIdType.MESH,
        )
        copy.start()
        copies.append(copy)
    total = part[pl.ds(pl.multiple_of(x * pair, 8), pair)]
    for i, copy in enumerate(copies):
        copy.wait_recv()
        total = total + arrived[i].astype(jnp.float32)
    mine[...] = total
    there = pl.multiple_of((1 - half) * share, 8)
    crossing[...] = mine[pl.ds(there, share)].astype(crossing.dtype)
    copy = pltpu.make_async_remote_copy(
        src_ref=crossing,
        dst_ref=other,
        send_sem=send2,
        recv_sem=recv2,
        device_id={"tp": across},
        device_id_type=pl.DeviceIdType.MESH,
    )
    copy.start()
    copy.wait_recv()
    here = pl.multiple_of(half * share, 8)
    out[...] = mine[pl.ds(here, share)] + other[...].astype(jnp.float32)
    for done in copies:
        done.wait_send()
    copy.wait_send()


def tp_sum(part, members):
    rows, width = part.shape
    share = rows // members
    sides = members // 2
    return pl.pallas_call(
        tp_sum_kernel,
        out_shape=jax.ShapeDtypeStruct((share, width), jnp.float32),
        in_specs=[whole(VMEM)],
        out_specs=whole(VMEM),
        scratch_shapes=[
            pltpu.VMEM((rows, width), jnp.bfloat16),
            pltpu.VMEM((sides - 1, 2 * share, width), jnp.bfloat16),
            pltpu.VMEM((2 * share, width), jnp.float32),
            pltpu.VMEM((share, width), jnp.bfloat16),
            pltpu.VMEM((share, width), jnp.bfloat16),
            pltpu.SemaphoreType.DMA((sides - 1,)),
            pltpu.SemaphoreType.DMA((sides - 1,)),
            pltpu.SemaphoreType.DMA,
            pltpu.SemaphoreType.DMA,
        ],
        compiler_params=pltpu.CompilerParams(
            collective_id=0, has_side_effects=True, vmem_limit_bytes=4 << 20
        ),
        cost_estimate=pl.CostEstimate(
            flops=0, transcendentals=0, bytes_accessed=4 << 20
        ),
        name="tp_sum",
    )(part)


def finish_kernel(live, requests, times, total, latent, velocity, latent_next):
    _, slots, share, ch = latent.shape
    groups = lax.axis_size("grp")
    group = lax.axis_index("grp")
    first = lax.axis_index("tp") * share
    pair = lax.rem(group, groups // 2)
    ids = first + lax.broadcasted_iota(jnp.int32, (share, ch), 0)
    for s in range(slots):
        request = requests[pair * slots + s]
        gap = times[1, request] - times[0, request]
        step = jnp.full((share, ch), gap, jnp.int32).astype(jnp.float32) / 1000.0
        v = jnp.where(ids < live[s, group], total[:, s * ch : (s + 1) * ch], 0.0)
        velocity[0, s] = v
        latent_next[0, s] = latent[0, s] + step * v


def finish(live_t, request_list, times_t, total, latent):
    return pl.pallas_call(
        finish_kernel,
        out_shape=(
            jax.ShapeDtypeStruct(latent.shape, jnp.float32),
            jax.ShapeDtypeStruct(latent.shape, jnp.float32),
        ),
        in_specs=[whole(SMEM)] * 3 + [whole(VMEM)] * 2,
        out_specs=(whole(VMEM), whole(VMEM)),
        compiler_params=pltpu.CompilerParams(vmem_limit_bytes=4 << 20),
        cost_estimate=pl.CostEstimate(
            flops=0, transcendentals=0, bytes_accessed=1 << 20
        ),
        name="finish",
    )(live_t, request_list, times_t, total, latent)


def in_order(array):
    return with_layout_constraint(array, Layout(tuple(range(array.ndim))))


def apart(kv):
    return jnp.transpose(kv[0], (0, 2, 1, 3))


def shards(
    queries,
    fresh_kv,
    stale_kv,
    text_kv,
    w_velocity,
    latent,
    live_counts,
    refresh_rows,
    request_list,
    timesteps,
):
    half_groups = lax.axis_size("grp") // 2
    live_t = live_counts.T
    times_t = timesteps.T
    rows = fresh_kv.shape[2]
    listed = refresh_rows.shape[2]
    text_other = in_order(from_behind(in_order(text_kv), "grp", half_groups))
    early_out, bulk_out = pack(refresh_rows, fresh_kv)
    early = from_behind(early_out, "grp", half_groups)
    bias, sub = prepare(refresh_rows, live_t, rows)
    text_other, bulk_out, bias, sub = lax.optimization_barrier(
        (text_other, bulk_out, bias, sub)
    )
    bulk = from_behind(bulk_out, "grp", half_groups)
    early_apart = jnp.pad(apart(early), ((0, 0), (0, 0), (0, TILE - listed), (0, 0)))
    part = attend(
        bias,
        queries,
        apart(fresh_kv),
        apart(stale_kv),
        apart(text_kv),
        apart(text_other),
        early_apart,
        w_velocity.T,
    )
    total = tp_sum(part, lax.axis_size("tp"))
    velocity, latent_next = finish(live_t, request_list, times_t, total, latent)
    next_stale = unpack(refresh_rows, sub, early, bulk, velocity)
    return next_stale, velocity, latent_next


def solution(mesh):
    return jax.shard_map(
        shards,
        mesh=mesh,
        in_specs=(
            P("grp", None, None, "tp"),
            P("grp", None, None, None, "tp"),
            P("grp", None, None, None, "tp"),
            P("grp", None, None, None, "tp"),
            P("tp", None),
            P("grp", None, "tp", None),
            P(),
            P(),
            P(),
            P(),
        ),
        out_specs=(
            P("grp", None, None, None, "tp"),
            P("grp", None, "tp", None),
            P("grp", None, "tp", None),
        ),
        check_vma=False,
    )
```

```python
import math

import jax
import jax.numpy as jnp
from jax import lax
from jax.experimental.layout import Layout, with_layout_constraint
from jax.experimental import pallas as pl
from jax.experimental.pallas import tpu as pltpu
from jax.sharding import PartitionSpec as P

HD = 128
TILE = 128
SCALE = math.log2(math.e) / math.sqrt(HD)
VMEM = pltpu.MemorySpace.VMEM
SMEM = pltpu.MemorySpace.SMEM
HBM = pltpu.MemorySpace.HBM


def whole(space):
    return pl.BlockSpec(memory_space=space)


def from_behind(block, axis, distance):
    devices = range(lax.axis_size(axis))
    route = [((i - distance) % len(devices), i) for i in devices]
    return lax.ppermute(block, axis, route)


def counted(mask, axis):
    return jnp.sum(jnp.where(mask, 1.0, 0.0), axis=axis, keepdims=True)


def exchange_rows(listed_row, rows):
    n = listed_row.shape[1]
    keep = float(rows - n)
    down = lax.broadcasted_iota(jnp.int32, (n, n), 0).astype(jnp.float32)
    along = lax.broadcasted_iota(jnp.int32, (n, n), 1).astype(jnp.float32)
    diagonal = down == along
    listed_col = jnp.sum(
        jnp.where(diagonal, listed_row, 0.0), axis=1, keepdims=True
    )
    used_row = counted(listed_col == along + keep, 0)
    used_col = counted(listed_row == down + keep, 1)
    free_rank = jnp.sum(
        jnp.where(down < along, 1.0 - used_col, 0.0), axis=0, keepdims=True
    )
    low_rank = counted(jnp.logical_and(along < down, listed_row < keep), 1)
    match = jnp.logical_and(low_rank == free_rank, used_row == 0.0)
    found = jnp.sum(jnp.where(match, along + keep, 0.0), axis=1, keepdims=True)
    found = jnp.where(listed_col < keep, found, listed_col)
    found_row = jnp.sum(jnp.where(diagonal, found, 0.0), axis=0, keepdims=True)
    return listed_col, found_row


def pack_kernel(
    lists, fresh, early, bulk, held, mine, plan, where, list_sem, plan_sem, in_sem, out_sem
):
    _, slots, rows, _, _ = fresh.shape
    listed = early.shape[2]
    keep = rows - listed
    step = 8
    group = lax.axis_index("grp")
    load_list = pltpu.make_async_copy(lists.at[group], mine, list_sem)
    load_list.start()
    loads = [
        pltpu.make_async_copy(fresh.at[0, s], held.at[s], in_sem.at[s])
        for s in range(slots)
    ]
    for load in loads:
        load.start()
    load_list.wait()
    for s in range(slots):
        listed_row = mine[s : s + 1, :]
        _, found = exchange_rows(listed_row.astype(jnp.float32), rows)
        plan[2 * s : 2 * s + 1, :listed] = listed_row
        plan[2 * s + 1 : 2 * s + 2, :listed] = found.astype(jnp.int32)
    move = pltpu.make_async_copy(plan, where, plan_sem)
    move.start()
    move.wait()
    stores = []
    for s in range(slots):
        loads[s].wait()

        def exchange(i, carry, s=s):
            ids = [i * step + k for k in range(step)]
            at = [where[2 * s, j] for j in ids]
            to = [where[2 * s + 1, j] for j in ids]
            taken = [held[s, row] for row in at]
            given = [held[s, row] for row in to]
            for k in range(step):
                early[0, s, ids[k]] = taken[k]
            for k in range(step):
                held[s, at[k]] = given[k]
            return carry

        lax.fori_loop(0, listed // step, exchange, 0)
        store = pltpu.make_async_copy(
            held.at[s, pl.ds(0, keep)], bulk.at[0, s], out_sem.at[s]
        )
        store.start()
        stores.append(store)
    for store in stores:
        store.wait()


def pack(refresh_rows, fresh_kv):
    _, slots, rows, two, width = fresh_kv.shape
    listed = refresh_rows.shape[2]
    keep = rows - listed
    kv = fresh_kv.dtype
    return pl.pallas_call(
        pack_kernel,
        out_shape=(
            jax.ShapeDtypeStruct((1, slots, listed, two, width), kv),
            jax.ShapeDtypeStruct((1, slots, keep, two, width), kv),
        ),
        in_specs=[whole(HBM), whole(HBM)],
        out_specs=(whole(VMEM), whole(pl.ANY)),
        scratch_shapes=[
            pltpu.VMEM((slots, rows, two, width), kv),
            pltpu.VMEM((slots, listed), jnp.int32),
            pltpu.VMEM((8, TILE), jnp.int32),
            pltpu.SMEM((8, TILE), jnp.int32),
            pltpu.SemaphoreType.DMA,
            pltpu.SemaphoreType.DMA,
            pltpu.SemaphoreType.DMA((slots,)),
            pltpu.SemaphoreType.DMA((slots,)),
        ],
        compiler_params=pltpu.CompilerParams(vmem_limit_bytes=8 << 20),
        cost_estimate=pl.CostEstimate(
            flops=0, transcendentals=0, bytes_accessed=4 << 20
        ),
        name="pack",
    )(refresh_rows, fresh_kv)


def unpack_kernel(
    where,
    early,
    bulk,
    total,
    shown,
    step_size,
    latent,
    out,
    velocity,
    latent_next,
    held,
    v_held,
    in_sem,
    out_sem,
    v_sem,
):
    _, slots, rows, _, _ = out.shape
    ch = latent.shape[3]
    listed = early.shape[2]
    keep = rows - listed
    step = 8
    loads = [
        pltpu.make_async_copy(
            bulk.at[0, s], held.at[s, pl.ds(0, keep)], in_sem.at[s]
        )
        for s in range(slots)
    ]
    for load in loads:
        load.start()
    for s in range(slots):
        v = jnp.where(shown[s] > 0.0, total[:, s * ch : (s + 1) * ch], 0.0)
        v_held[0, s] = v
        v_held[1, s] = latent[0, s] + step_size[s] * v
    stores = [
        pltpu.make_async_copy(v_held.at[i], ref.at[0], v_sem.at[i])
        for i, ref in enumerate((velocity, latent_next))
    ]
    for store in stores:
        store.start()
    for s in range(slots):
        loads[s].wait()

        def place(i, carry, s=s):
            ids = [i * step + k for k in range(step)]
            at = [where[2 * s, j] for j in ids]
            to = [where[2 * s + 1, j] for j in ids]
            moved = [held[s, row] for row in at]
            new = [early[0, s, j] for j in ids]
            for k in range(step):
                held[s, to[k]] = moved[k]
            for k in range(step):
                held[s, at[k]] = new[k]
            return carry

        lax.fori_loop(0, listed // step, place, 0)
        store = pltpu.make_async_copy(held.at[s], out.at[0, s], out_sem.at[s])
        store.start()
        stores.append(store)
    for store in stores:
        store.wait()


def unpack(where, early, bulk, total, shown, step_size, latent):
    _, slots, listed, two, width = early.shape
    rows = bulk.shape[2] + listed
    kv = bulk.dtype
    return pl.pallas_call(
        unpack_kernel,
        out_shape=(
            jax.ShapeDtypeStruct((1, slots, rows, two, width), kv),
            jax.ShapeDtypeStruct(latent.shape, jnp.float32),
            jax.ShapeDtypeStruct(latent.shape, jnp.float32),
        ),
        in_specs=[whole(SMEM), whole(VMEM), whole(pl.ANY)] + [whole(VMEM)] * 4,
        out_specs=(whole(pl.ANY), whole(HBM), whole(HBM)),
        scratch_shapes=[
            pltpu.VMEM((slots, rows, two, width), kv),
            pltpu.VMEM((2,) + latent.shape[1:], jnp.float32),
            pltpu.SemaphoreType.DMA((slots,)),
            pltpu.SemaphoreType.DMA((slots,)),
            pltpu.SemaphoreType.DMA((2,)),
        ],
        compiler_params=pltpu.CompilerParams(vmem_limit_bytes=8 << 20),
        cost_estimate=pl.CostEstimate(
            flops=0, transcendentals=0, bytes_accessed=4 << 20
        ),
        name="unpack",
    )(where, early, bulk, total, shown, step_size, latent)


def prepare_kernel(
    lists, live, requests, times, bias, where, shown, step, theirs, list_sem
):
    slots = bias.shape[0]
    listed = lists.shape[2]
    rows = (bias.shape[2] - TILE) // 2
    groups = lax.axis_size("grp")
    group = lax.axis_index("grp")
    partner = lax.rem(group + groups // 2, groups)
    load_list = pltpu.make_async_copy(lists.at[partner], theirs, list_sem)
    load_list.start()
    ids = lax.broadcasted_iota(jnp.int32, (1, rows), 1)
    ids_down = lax.broadcasted_iota(jnp.int32, (listed, rows), 1).astype(jnp.float32)
    dead = jnp.float32(-jnp.inf)
    load_list.wait()
    for s in range(slots):
        partner_live = live[s, partner]
        listed_row = theirs[s : s + 1, :]
        listed_col, found = exchange_rows(listed_row.astype(jnp.float32), rows)
        where[2 * s : 2 * s + 1, :listed] = listed_row
        where[2 * s + 1 : 2 * s + 2, :listed] = found.astype(jnp.int32)
        replaced = counted(ids_down == listed_col, 0) > 0.0
        counts = jnp.logical_and(ids < partner_live, jnp.logical_not(replaced))
        bias[s, :, :rows] = jnp.where(ids < live[s, group], 0.0, dead)
        bias[s, :, rows : 2 * rows] = jnp.where(counts, 0.0, dead)
        bias[s, :, 2 * rows :] = jnp.full((1, TILE), dead)
        bias[s, :, 2 * rows : 2 * rows + listed] = jnp.where(
            listed_row < partner_live, 0.0, dead
        )
    _, share, ch = shown.shape
    share_ids = lax.axis_index("tp") * share + lax.broadcasted_iota(
        jnp.int32, (share, ch), 0
    )
    pair = lax.rem(group, groups // 2)
    for s in range(slots):
        request = requests[pair * slots + s]
        gap = times[1, request] - times[0, request]
        shown[s] = jnp.where(share_ids < live[s, group], 1.0, 0.0)
        step[s] = jnp.full((share, ch), gap, jnp.int32).astype(jnp.float32) / 1000.0


def prepare(refresh_rows, live_t, request_list, times_t, rows, latent):
    _, slots, listed = refresh_rows.shape
    aside = jax.ShapeDtypeStruct(latent.shape[1:], jnp.float32)
    return pl.pallas_call(
        prepare_kernel,
        out_shape=(
            jax.ShapeDtypeStruct((slots, 1, 2 * rows + TILE), jnp.float32),
            jax.ShapeDtypeStruct((8, TILE), jnp.int32),
            aside,
            aside,
        ),
        in_specs=[whole(HBM), whole(SMEM), whole(SMEM), whole(SMEM)],
        out_specs=(whole(VMEM),) * 4,
        scratch_shapes=[
            pltpu.VMEM((slots, listed), jnp.int32),
            pltpu.SemaphoreType.DMA,
        ],
        compiler_params=pltpu.CompilerParams(vmem_limit_bytes=4 << 20),
        cost_estimate=pl.CostEstimate(
            flops=0, transcendentals=0, bytes_accessed=1 << 20
        ),
        name="prepare",
    )(refresh_rows, live_t, request_list, times_t)


def tiles(array):
    return [array[:, i : i + TILE] for i in range(0, array.shape[1], TILE)]


def attend_kernel(bias, q, own, stale, text, text_other, early, w_t, out, scores):
    slot = pl.program_id(0)
    rows = own.shape[2]
    heads = q.shape[3] // HD
    part_rows = scores.shape[1]
    ch = w_t.shape[0]
    blocks = (
        (own, 0, bias[0, :, :rows]),
        (stale, rows, bias[0, :, rows : 2 * rows]),
        (early, 2 * rows, bias[0, :, 2 * rows :]),
        (text, 2 * rows + TILE, None),
        (text_other, 2 * rows + TILE + text.shape[2], None),
    )

    def score(unit, place, block, top):
        head, first = unit
        kv, at, block_bias = block
        s = lax.dot_general(
            q[0, 0, first : first + part_rows, head * HD : (head + 1) * HD],
            kv[0, 0, :, head * HD : (head + 1) * HD],
            (((1,), (1,)), ((), ())),
            preferred_element_type=jnp.float32,
        )
        if block_bias is not None:
            s = s + block_bias
        scores[place, :, at : at + s.shape[1]] = s
        for tile in tiles(s):
            top = tile if top is None else jnp.maximum(top, tile)
        return top

    def weigh(unit, place, block, shift, total, blended):
        head, _ = unit
        kv, at, _ = block
        weights = jnp.exp2(
            scores[place, :, at : at + kv.shape[2]] * SCALE - shift
        )
        for tile in tiles(weights):
            total = tile if total is None else total + tile
        part = jnp.dot(
            weights.astype(jnp.bfloat16),
            kv[0, 1, :, head * HD : (head + 1) * HD],
            preferred_element_type=jnp.float32,
        )
        return total, part if blended is None else blended + part

    units = [
        (head, first)
        for first in range(0, rows, part_rows)
        for head in range(heads)
    ]
    top = None
    for block in blocks:
        top = score(units[0], 0, block, top)
    velocity = {}
    for i, unit in enumerate(units):
        shift = jnp.max(top, axis=1, keepdims=True) * SCALE
        top = total = blended = None
        for block in blocks:
            if i + 1 < len(units):
                top = score(units[i + 1], (i + 1) % 2, block, top)
            total, blended = weigh(unit, i % 2, block, shift, total, blended)
        total = jnp.sum(total, axis=1, keepdims=True)
        head, first = unit
        v = lax.dot_general(
            (blended / total).astype(jnp.bfloat16),
            w_t[:, head * HD : (head + 1) * HD],
            (((1,), (1,)), ((), ())),
            preferred_element_type=jnp.float32,
        )
        velocity[first] = v if first not in velocity else velocity[first] + v

    for s in range(2):

        @pl.when(slot == s)
        def _(s=s):
            for first, v in velocity.items():
                out[first : first + part_rows, s * ch : (s + 1) * ch] = v


def attend(bias, queries, own, stale, text, text_other, early, w_t):
    _, slots, rows, inner = queries.shape
    ch = w_t.shape[0]
    keys = sum(a.shape[2] for a in (own, stale, text, text_other, early))

    def kv_spec(a):
        return pl.BlockSpec((1, 2, a.shape[2], inner), lambda s: (s, 0, 0, 0))

    return pl.pallas_call(
        attend_kernel,
        grid=(slots,),
        out_shape=jax.ShapeDtypeStruct((rows, slots * ch), jnp.float32),
        in_specs=[
            pl.BlockSpec((1, 1, bias.shape[2]), lambda s: (s, 0, 0)),
            pl.BlockSpec((1, 1, rows, inner), lambda s: (0, s, 0, 0)),
            kv_spec(own),
            kv_spec(stale),
            kv_spec(text),
            kv_spec(text_other),
            kv_spec(early),
            pl.BlockSpec((ch, inner), lambda s: (0, 0)),
        ],
        out_specs=pl.BlockSpec((rows, slots * ch), lambda s: (0, 0)),
        scratch_shapes=[pltpu.VMEM((2, rows // 2, keys), jnp.float32)],
        compiler_params=pltpu.CompilerParams(vmem_limit_bytes=24 << 20),
        cost_estimate=pl.CostEstimate(
            flops=20 * slots * rows * keys * inner,
            transcendentals=slots * rows * keys * inner // HD,
            bytes_accessed=4 << 20,
        ),
        name="attend",
    )(bias, queries, own, stale, text, text_other, early, w_t)


def tp_sum_kernel(
    part, out, leaving, arrived, mine, crossing, other, send, recv, send2, recv2
):
    t = lax.axis_index("tp")
    x, half = t // 2, lax.rem(t, 2)
    sides = lax.axis_size("tp") // 2
    share = out.shape[0]
    pair = 2 * share
    peers = [lax.rem(x + d, sides) for d in range(1, sides)]
    across = x * 2 + 1 - half

    barrier = pltpu.get_barrier_semaphore()
    for peer in peers:
        pl.semaphore_signal(
            barrier,
            inc=1,
            device_id={"tp": peer * 2 + half},
            device_id_type=pl.DeviceIdType.MESH,
        )
    pl.semaphore_signal(
        barrier,
        inc=1,
        device_id={"tp": across},
        device_id_type=pl.DeviceIdType.MESH,
    )
    leaving[...] = part[...].astype(leaving.dtype)
    pl.semaphore_wait(barrier, sides)

    copies = []
    for i, peer in enumerate(peers):
        copy = pltpu.make_async_remote_copy(
            src_ref=leaving.at[pl.ds(pl.multiple_of(peer * pair, 16), pair)],
            dst_ref=arrived.at[i],
            send_sem=send.at[i],
            recv_sem=recv.at[i],
            device_id={"tp": peer * 2 + half},
            device_id_type=pl.DeviceIdType.MESH,
        )
        copy.start()
        copies.append(copy)
    total = part[pl.ds(pl.multiple_of(x * pair, 8), pair)]
    for i, copy in enumerate(copies):
        copy.wait_recv()
        total = total + arrived[i].astype(jnp.float32)
    mine[...] = total
    there = pl.multiple_of((1 - half) * share, 8)
    crossing[...] = mine[pl.ds(there, share)].astype(crossing.dtype)
    copy = pltpu.make_async_remote_copy(
        src_ref=crossing,
        dst_ref=other,
        send_sem=send2,
        recv_sem=recv2,
        device_id={"tp": across},
        device_id_type=pl.DeviceIdType.MESH,
    )
    copy.start()
    copy.wait_recv()
    here = pl.multiple_of(half * share, 8)
    out[...] = mine[pl.ds(here, share)] + other[...].astype(jnp.float32)
    for done in copies:
        done.wait_send()
    copy.wait_send()


def tp_sum(part, members):
    rows, width = part.shape
    share = rows // members
    sides = members // 2
    return pl.pallas_call(
        tp_sum_kernel,
        out_shape=jax.ShapeDtypeStruct((share, width), jnp.float32),
        in_specs=[whole(VMEM)],
        out_specs=whole(VMEM),
        scratch_shapes=[
            pltpu.VMEM((rows, width), jnp.bfloat16),
            pltpu.VMEM((sides - 1, 2 * share, width), jnp.bfloat16),
            pltpu.VMEM((2 * share, width), jnp.float32),
            pltpu.VMEM((share, width), jnp.bfloat16),
            pltpu.VMEM((share, width), jnp.bfloat16),
            pltpu.SemaphoreType.DMA((sides - 1,)),
            pltpu.SemaphoreType.DMA((sides - 1,)),
            pltpu.SemaphoreType.DMA,
            pltpu.SemaphoreType.DMA,
        ],
        compiler_params=pltpu.CompilerParams(
            collective_id=0, has_side_effects=True, vmem_limit_bytes=4 << 20
        ),
        cost_estimate=pl.CostEstimate(
            flops=0, transcendentals=0, bytes_accessed=4 << 20
        ),
        name="tp_sum",
    )(part)


def in_order(array):
    return with_layout_constraint(array, Layout(tuple(range(array.ndim))))


def apart(kv):
    return jnp.transpose(kv[0], (0, 2, 1, 3))


def shards(
    queries,
    fresh_kv,
    stale_kv,
    text_kv,
    w_velocity,
    latent,
    live_counts,
    refresh_rows,
    request_list,
    timesteps,
):
    half_groups = lax.axis_size("grp") // 2
    live_t = live_counts.T
    times_t = timesteps.T
    rows = fresh_kv.shape[2]
    listed = refresh_rows.shape[2]
    text_other = in_order(from_behind(in_order(text_kv), "grp", half_groups))
    early_out, bulk_out = pack(refresh_rows, fresh_kv)
    early = from_behind(early_out, "grp", half_groups)
    bias, where, shown, step_size = prepare(
        refresh_rows, live_t, request_list, times_t, rows, latent
    )
    text_other, bulk_out, bias, where = lax.optimization_barrier(
        (text_other, bulk_out, bias, where)
    )
    bulk = from_behind(bulk_out, "grp", half_groups)
    early_apart = jnp.pad(apart(early), ((0, 0), (0, 0), (0, TILE - listed), (0, 0)))
    part = attend(
        bias,
        queries,
        apart(fresh_kv),
        apart(stale_kv),
        apart(text_kv),
        apart(text_other),
        early_apart,
        w_velocity.T,
    )
    total = tp_sum(part, lax.axis_size("tp"))
    return unpack(where, early, bulk, total, shown, step_size, latent)


def solution(mesh):
    return jax.shard_map(
        shards,
        mesh=mesh,
        in_specs=(
            P("grp", None, None, "tp"),
            P("grp", None, None, None, "tp"),
            P("grp", None, None, None, "tp"),
            P("grp", None, None, None, "tp"),
            P("tp", None),
            P("grp", None, "tp", None),
            P(),
            P(),
            P(),
            P(),
        ),
        out_specs=(
            P("grp", None, None, None, "tp"),
            P("grp", None, "tp", None),
            P("grp", None, "tp", None),
        ),
        check_vma=False,
    )
```

```python
import math

import jax
import jax.numpy as jnp
from jax import lax
from jax.experimental.layout import Layout, with_layout_constraint
from jax.experimental import pallas as pl
from jax.experimental.pallas import tpu as pltpu
from jax.sharding import PartitionSpec as P

HD = 128
TILE = 128
SCALE = math.log2(math.e) / math.sqrt(HD)
VMEM = pltpu.MemorySpace.VMEM
SMEM = pltpu.MemorySpace.SMEM
HBM = pltpu.MemorySpace.HBM


def whole(space):
    return pl.BlockSpec(memory_space=space)


def from_behind(block, axis, distance):
    devices = range(lax.axis_size(axis))
    route = [((i - distance) % len(devices), i) for i in devices]
    return lax.ppermute(block, axis, route)


def counted(mask, axis):
    return jnp.sum(jnp.where(mask, 1.0, 0.0), axis=axis, keepdims=True)


def exchange_rows(listed_row, rows):
    n = listed_row.shape[1]
    keep = float(rows - n)
    down = lax.broadcasted_iota(jnp.int32, (n, n), 0).astype(jnp.float32)
    along = lax.broadcasted_iota(jnp.int32, (n, n), 1).astype(jnp.float32)
    diagonal = down == along
    listed_col = jnp.sum(
        jnp.where(diagonal, listed_row, 0.0), axis=1, keepdims=True
    )
    used_row = counted(listed_col == along + keep, 0)
    used_col = counted(listed_row == down + keep, 1)
    free_rank = jnp.sum(
        jnp.where(down < along, 1.0 - used_col, 0.0), axis=0, keepdims=True
    )
    low_rank = counted(jnp.logical_and(along < down, listed_row < keep), 1)
    match = jnp.logical_and(low_rank == free_rank, used_row == 0.0)
    found = jnp.sum(jnp.where(match, along + keep, 0.0), axis=1, keepdims=True)
    found = jnp.where(listed_col < keep, found, listed_col)
    found_row = jnp.sum(jnp.where(diagonal, found, 0.0), axis=0, keepdims=True)
    return listed_col, found_row


def pack_kernel(
    lists, fresh, early, bulk, held, mine, plan, where, list_sem, plan_sem, in_sem, out_sem
):
    _, slots, rows, _, _ = fresh.shape
    listed = early.shape[2]
    keep = rows - listed
    step = 8
    group = lax.axis_index("grp")
    load_list = pltpu.make_async_copy(lists.at[group], mine, list_sem)
    load_list.start()
    loads = [
        pltpu.make_async_copy(fresh.at[0, s], held.at[s], in_sem.at[s])
        for s in range(slots)
    ]
    for load in loads:
        load.start()
    load_list.wait()
    for s in range(slots):
        listed_row = mine[s : s + 1, :]
        _, found = exchange_rows(listed_row.astype(jnp.float32), rows)
        plan[2 * s : 2 * s + 1, :listed] = listed_row
        plan[2 * s + 1 : 2 * s + 2, :listed] = found.astype(jnp.int32)
    move = pltpu.make_async_copy(plan, where, plan_sem)
    move.start()
    move.wait()
    stores = []
    for s in range(slots):
        loads[s].wait()

        def exchange(i, carry, s=s):
            ids = [i * step + k for k in range(step)]
            at = [where[2 * s, j] for j in ids]
            to = [where[2 * s + 1, j] for j in ids]
            taken = [held[s, row] for row in at]
            given = [held[s, row] for row in to]
            for k in range(step):
                early[0, s, ids[k]] = taken[k]
            for k in range(step):
                held[s, at[k]] = given[k]
            return carry

        lax.fori_loop(0, listed // step, exchange, 0)
        store = pltpu.make_async_copy(
            held.at[s, pl.ds(0, keep)], bulk.at[0, s], out_sem.at[s]
        )
        store.start()
        stores.append(store)
    for store in stores:
        store.wait()


def pack(refresh_rows, fresh_kv):
    _, slots, rows, two, width = fresh_kv.shape
    listed = refresh_rows.shape[2]
    keep = rows - listed
    kv = fresh_kv.dtype
    return pl.pallas_call(
        pack_kernel,
        out_shape=(
            jax.ShapeDtypeStruct((1, slots, listed, two, width), kv),
            jax.ShapeDtypeStruct((1, slots, keep, two, width), kv),
        ),
        in_specs=[whole(HBM), whole(HBM)],
        out_specs=(whole(VMEM), whole(pl.ANY)),
        scratch_shapes=[
            pltpu.VMEM((slots, rows, two, width), kv),
            pltpu.VMEM((slots, listed), jnp.int32),
            pltpu.VMEM((8, TILE), jnp.int32),
            pltpu.SMEM((8, TILE), jnp.int32),
            pltpu.SemaphoreType.DMA,
            pltpu.SemaphoreType.DMA,
            pltpu.SemaphoreType.DMA((slots,)),
            pltpu.SemaphoreType.DMA((slots,)),
        ],
        compiler_params=pltpu.CompilerParams(vmem_limit_bytes=8 << 20),
        cost_estimate=pl.CostEstimate(
            flops=0, transcendentals=0, bytes_accessed=4 << 20
        ),
        name="pack",
    )(refresh_rows, fresh_kv)


def unpack_kernel(where, early, bulk, out, passed, held, in_sem, out_sem):
    passed[...] = jnp.zeros_like(passed)
    _, slots, rows, _, _ = out.shape
    listed = early.shape[2]
    keep = rows - listed
    step = 8
    loads = [
        pltpu.make_async_copy(
            bulk.at[0, s], held.at[s, pl.ds(0, keep)], in_sem.at[s]
        )
        for s in range(slots)
    ]
    for load in loads:
        load.start()
    stores = []
    for s in range(slots):
        loads[s].wait()

        def place(i, carry, s=s):
            ids = [i * step + k for k in range(step)]
            at = [where[2 * s, j] for j in ids]
            to = [where[2 * s + 1, j] for j in ids]
            moved = [held[s, row] for row in at]
            new = [early[0, s, j] for j in ids]
            for k in range(step):
                held[s, to[k]] = moved[k]
            for k in range(step):
                held[s, at[k]] = new[k]
            return carry

        lax.fori_loop(0, listed // step, place, 0)
        store = pltpu.make_async_copy(held.at[s], out.at[0, s], out_sem.at[s])
        store.start()
        stores.append(store)
    for store in stores:
        store.wait()


def unpack(where, early, bulk):
    _, slots, listed, two, width = early.shape
    rows = bulk.shape[2] + listed
    kv = bulk.dtype
    return pl.pallas_call(
        unpack_kernel,
        out_shape=(
            jax.ShapeDtypeStruct((1, slots, rows, two, width), kv),
            jax.ShapeDtypeStruct((8, TILE), jnp.float32),
        ),
        in_specs=[whole(SMEM), whole(VMEM), whole(pl.ANY)],
        out_specs=(whole(pl.ANY), whole(VMEM)),
        scratch_shapes=[
            pltpu.VMEM((slots, rows, two, width), kv),
            pltpu.SemaphoreType.DMA((slots,)),
            pltpu.SemaphoreType.DMA((slots,)),
        ],
        compiler_params=pltpu.CompilerParams(vmem_limit_bytes=8 << 20),
        cost_estimate=pl.CostEstimate(
            flops=0, transcendentals=0, bytes_accessed=4 << 20
        ),
        name="unpack",
    )(where, early, bulk)


def finish_kernel(kept, other, shown, step_size, latent, after, velocity, latent_next):
    _, slots, _, ch = latent.shape
    total = kept[...] + other[...].astype(jnp.float32)
    for s in range(slots):
        v = jnp.where(shown[s] > 0.0, total[:, s * ch : (s + 1) * ch], 0.0)
        velocity[0, s] = v
        latent_next[0, s] = latent[0, s] + step_size[s] * v


def finish(kept, other, shown, step_size, latent, after):
    return pl.pallas_call(
        finish_kernel,
        out_shape=(jax.ShapeDtypeStruct(latent.shape, jnp.float32),) * 2,
        in_specs=[whole(VMEM)] * 6,
        out_specs=(whole(VMEM),) * 2,
        compiler_params=pltpu.CompilerParams(vmem_limit_bytes=4 << 20),
        cost_estimate=pl.CostEstimate(
            flops=0, transcendentals=0, bytes_accessed=1 << 18
        ),
        name="finish",
    )(kept, other, shown, step_size, latent, after)


def prepare_kernel(
    lists, live, requests, times, bias, where, shown, step, theirs, list_sem
):
    slots = bias.shape[0]
    listed = lists.shape[2]
    rows = (bias.shape[2] - TILE) // 2
    groups = lax.axis_size("grp")
    group = lax.axis_index("grp")
    partner = lax.rem(group + groups // 2, groups)
    load_list = pltpu.make_async_copy(lists.at[partner], theirs, list_sem)
    load_list.start()
    ids = lax.broadcasted_iota(jnp.int32, (1, rows), 1)
    ids_down = lax.broadcasted_iota(jnp.int32, (listed, rows), 1).astype(jnp.float32)
    dead = jnp.float32(-jnp.inf)
    load_list.wait()
    for s in range(slots):
        partner_live = live[s, partner]
        listed_row = theirs[s : s + 1, :]
        listed_col, found = exchange_rows(listed_row.astype(jnp.float32), rows)
        where[2 * s : 2 * s + 1, :listed] = listed_row
        where[2 * s + 1 : 2 * s + 2, :listed] = found.astype(jnp.int32)
        replaced = counted(ids_down == listed_col, 0) > 0.0
        counts = jnp.logical_and(ids < partner_live, jnp.logical_not(replaced))
        bias[s, :, :rows] = jnp.where(ids < live[s, group], 0.0, dead)
        bias[s, :, rows : 2 * rows] = jnp.where(counts, 0.0, dead)
        bias[s, :, 2 * rows :] = jnp.full((1, TILE), dead)
        bias[s, :, 2 * rows : 2 * rows + listed] = jnp.where(
            listed_row < partner_live, 0.0, dead
        )
    _, share, ch = shown.shape
    share_ids = lax.axis_index("tp") * share + lax.broadcasted_iota(
        jnp.int32, (share, ch), 0
    )
    pair = lax.rem(group, groups // 2)
    for s in range(slots):
        request = requests[pair * slots + s]
        gap = times[1, request] - times[0, request]
        shown[s] = jnp.where(share_ids < live[s, group], 1.0, 0.0)
        step[s] = jnp.full((share, ch), gap, jnp.int32).astype(jnp.float32) / 1000.0


def prepare(refresh_rows, live_t, request_list, times_t, rows, latent):
    _, slots, listed = refresh_rows.shape
    aside = jax.ShapeDtypeStruct(latent.shape[1:], jnp.float32)
    return pl.pallas_call(
        prepare_kernel,
        out_shape=(
            jax.ShapeDtypeStruct((slots, 1, 2 * rows + TILE), jnp.float32),
            jax.ShapeDtypeStruct((8, TILE), jnp.int32),
            aside,
            aside,
        ),
        in_specs=[whole(HBM), whole(SMEM), whole(SMEM), whole(SMEM)],
        out_specs=(whole(VMEM),) * 4,
        scratch_shapes=[
            pltpu.VMEM((slots, listed), jnp.int32),
            pltpu.SemaphoreType.DMA,
        ],
        compiler_params=pltpu.CompilerParams(vmem_limit_bytes=4 << 20),
        cost_estimate=pl.CostEstimate(
            flops=0, transcendentals=0, bytes_accessed=1 << 20
        ),
        name="prepare",
    )(refresh_rows, live_t, request_list, times_t)


def tiles(array):
    return [array[:, i : i + TILE] for i in range(0, array.shape[1], TILE)]


def attend_kernel(
    bias,
    q,
    own,
    stale,
    text,
    text_other,
    early,
    w_t,
    kept,
    away,
    scores,
    packed,
    leaving,
    arrived,
    send,
    recv,
):
    slot = pl.program_id(0)
    t = lax.axis_index("tp")
    x, half = t // 2, lax.rem(t, 2)
    sides = lax.axis_size("tp") // 2
    share = kept.shape[0]
    peers = [lax.rem(x + d, sides) * 2 + half for d in range(1, sides)]

    def along_x(s, i):
        at = pl.multiple_of(peers[i] // 2 * share, share)
        return pltpu.make_async_remote_copy(
            src_ref=leaving.at[s, pl.ds(at, share)],
            dst_ref=arrived.at[s, i],
            send_sem=send.at[s, i],
            recv_sem=recv.at[s, i],
            device_id={"tp": peers[i]},
            device_id_type=pl.DeviceIdType.MESH,
        )

    barrier = pltpu.get_barrier_semaphore()

    @pl.when(slot == 0)
    def _():
        for peer in peers:
            pl.semaphore_signal(
                barrier,
                inc=1,
                device_id={"tp": peer},
                device_id_type=pl.DeviceIdType.MESH,
            )

    rows = own.shape[2]
    heads = q.shape[3] // HD
    part_rows = scores.shape[1]
    ch = w_t.shape[0]
    blocks = (
        (own, 0, bias[0, :, :rows]),
        (stale, rows, bias[0, :, rows : 2 * rows]),
        (early, 2 * rows, bias[0, :, 2 * rows :]),
        (text, 2 * rows + TILE, None),
        (text_other, 2 * rows + TILE + text.shape[2], None),
    )

    def score(unit, place, block, top):
        head, first = unit
        kv, at, block_bias = block
        s = lax.dot_general(
            q[0, 0, first : first + part_rows, head * HD : (head + 1) * HD],
            kv[0, 0, :, head * HD : (head + 1) * HD],
            (((1,), (1,)), ((), ())),
            preferred_element_type=jnp.float32,
        )
        if block_bias is not None:
            s = s + block_bias
        scores[place, :, at : at + s.shape[1]] = s
        for tile in tiles(s):
            top = tile if top is None else jnp.maximum(top, tile)
        return top

    def weigh(unit, place, block, shift, total, blended):
        head, _ = unit
        kv, at, _ = block
        weights = jnp.exp2(
            scores[place, :, at : at + kv.shape[2]] * SCALE - shift
        )
        for tile in tiles(weights):
            total = tile if total is None else total + tile
        part = jnp.dot(
            weights.astype(jnp.bfloat16),
            kv[0, 1, :, head * HD : (head + 1) * HD],
            preferred_element_type=jnp.float32,
        )
        return total, part if blended is None else blended + part

    units = [
        (head, first)
        for first in range(0, rows, part_rows)
        for head in range(heads)
    ]
    top = None
    for block in blocks:
        top = score(units[0], 0, block, top)
    velocity = {}
    for i, unit in enumerate(units):
        shift = jnp.max(top, axis=1, keepdims=True) * SCALE
        top = total = blended = None
        for block in blocks:
            if i + 1 < len(units):
                top = score(units[i + 1], (i + 1) % 2, block, top)
            total, blended = weigh(unit, i % 2, block, shift, total, blended)
        total = jnp.sum(total, axis=1, keepdims=True)
        head, first = unit
        v = lax.dot_general(
            (blended / total).astype(jnp.bfloat16),
            w_t[:, head * HD : (head + 1) * HD],
            (((1,), (1,)), ((), ())),
            preferred_element_type=jnp.float32,
        )
        velocity[first] = v if first not in velocity else velocity[first] + v

    for first, v in velocity.items():
        for at in range(0, part_rows, 2 * share):
            both = jnp.concatenate(
                [v[at : at + share], v[at + share : at + 2 * share]], axis=1
            )
            to = (first + at) // 2
            packed[slot, to : to + share] = both
            leaving[slot, to : to + share] = both.astype(leaving.dtype)

    @pl.when(slot == 0)
    def _():
        pl.semaphore_wait(barrier, sides - 1)

    for i in range(sides - 1):
        along_x(slot, i).start()

    @pl.when(slot == pl.num_programs(0) - 1)
    def _():
        for s in range(arrived.shape[0]):
            total = packed[s, pl.ds(pl.multiple_of(x * share, share), share)]
            for i in range(sides - 1):
                along_x(s, i).wait_recv()
                total = total + arrived[s, i].astype(jnp.float32)
            low, high = total[:, :ch], total[:, ch:]
            lanes = slice(s * ch, (s + 1) * ch)
            kept[:, lanes] = jnp.where(half == 0, low, high)
            away[:, lanes] = jnp.where(half == 0, high, low).astype(away.dtype)
        for s in range(arrived.shape[0]):
            for i in range(sides - 1):
                along_x(s, i).wait_send()


def attend(bias, queries, own, stale, text, text_other, early, w_t, members):
    _, slots, rows, inner = queries.shape
    ch = w_t.shape[0]
    keys = sum(a.shape[2] for a in (own, stale, text, text_other, early))
    share, sides = rows // members, members // 2
    sent = jnp.bfloat16

    def kv_spec(a):
        return pl.BlockSpec((1, 2, a.shape[2], inner), lambda s: (s, 0, 0, 0))

    return pl.pallas_call(
        attend_kernel,
        grid=(slots,),
        out_shape=(
            jax.ShapeDtypeStruct((share, slots * ch), jnp.float32),
            jax.ShapeDtypeStruct((share, slots * ch), sent),
        ),
        in_specs=[
            pl.BlockSpec((1, 1, bias.shape[2]), lambda s: (s, 0, 0)),
            pl.BlockSpec((1, 1, rows, inner), lambda s: (0, s, 0, 0)),
            kv_spec(own),
            kv_spec(stale),
            kv_spec(text),
            kv_spec(text_other),
            kv_spec(early),
            pl.BlockSpec((ch, inner), lambda s: (0, 0)),
        ],
        out_specs=(pl.BlockSpec((share, slots * ch), lambda s: (0, 0)),) * 2,
        scratch_shapes=[
            pltpu.VMEM((2, rows // 2, keys), jnp.float32),
            pltpu.VMEM((slots, rows // 2, 2 * ch), jnp.float32),
            pltpu.VMEM((slots, rows // 2, 2 * ch), sent),
            pltpu.VMEM((slots, sides - 1, share, 2 * ch), sent),
            pltpu.SemaphoreType.DMA((slots, sides - 1)),
            pltpu.SemaphoreType.DMA((slots, sides - 1)),
        ],
        compiler_params=pltpu.CompilerParams(
            collective_id=0, has_side_effects=True, vmem_limit_bytes=24 << 20
        ),
        cost_estimate=pl.CostEstimate(
            flops=40 * slots * rows * keys * inner,
            transcendentals=slots * rows * keys * inner // HD,
            bytes_accessed=4 << 20,
        ),
        name="attend",
    )(bias, queries, own, stale, text, text_other, early, w_t)


def in_order(array):
    return with_layout_constraint(array, Layout(tuple(range(array.ndim))))


def apart(kv):
    return jnp.transpose(kv[0], (0, 2, 1, 3))


def shards(
    queries,
    fresh_kv,
    stale_kv,
    text_kv,
    w_velocity,
    latent,
    live_counts,
    refresh_rows,
    request_list,
    timesteps,
):
    half_groups = lax.axis_size("grp") // 2
    live_t = live_counts.T
    times_t = timesteps.T
    rows = fresh_kv.shape[2]
    listed = refresh_rows.shape[2]
    text_other = in_order(from_behind(in_order(text_kv), "grp", half_groups))
    early_out, bulk_out = pack(refresh_rows, fresh_kv)
    early = in_order(from_behind(in_order(early_out), "grp", half_groups))
    bias, where, shown, step_size = prepare(
        refresh_rows, live_t, request_list, times_t, rows, latent
    )
    bulk_out, bias, where = lax.optimization_barrier((bulk_out, bias, where))
    bulk = from_behind(bulk_out, "grp", half_groups)
    early_apart = jnp.pad(apart(early), ((0, 0), (0, 0), (0, TILE - listed), (0, 0)))
    kept, away = attend(
        bias,
        queries,
        apart(fresh_kv),
        apart(stale_kv),
        apart(text_kv),
        apart(text_other),
        early_apart,
        w_velocity.T,
        lax.axis_size("tp"),
    )
    members = range(lax.axis_size("tp"))
    other = lax.ppermute(away, "tp", [(i, i ^ 1) for i in members])
    next_stale, passed = unpack(where, early, bulk)
    velocity, latent_next = finish(
        kept, other, shown, step_size, latent, passed
    )
    return next_stale, velocity, latent_next


def solution(mesh):
    return jax.shard_map(
        shards,
        mesh=mesh,
        in_specs=(
            P("grp", None, None, "tp"),
            P("grp", None, None, None, "tp"),
            P("grp", None, None, None, "tp"),
            P("grp", None, None, None, "tp"),
            P("tp", None),
            P("grp", None, "tp", None),
            P(),
            P(),
            P(),
            P(),
        ),
        out_specs=(
            P("grp", None, None, None, "tp"),
            P("grp", None, "tp", None),
            P("grp", None, "tp", None),
        ),
        check_vma=False,
    )
```

```python
import math

import jax
import jax.numpy as jnp
from jax import lax
from jax.experimental.layout import Layout, with_layout_constraint
from jax.experimental import pallas as pl
from jax.experimental.pallas import tpu as pltpu
from jax.sharding import PartitionSpec as P

HD = 128
TILE = 128
SCALE = math.log2(math.e) / math.sqrt(HD)
VMEM = pltpu.MemorySpace.VMEM
SMEM = pltpu.MemorySpace.SMEM
HBM = pltpu.MemorySpace.HBM


def whole(space):
    return pl.BlockSpec(memory_space=space)


def from_behind(block, axis, distance):
    devices = range(lax.axis_size(axis))
    route = [((i - distance) % len(devices), i) for i in devices]
    return lax.ppermute(block, axis, route)


def counted(mask, axis):
    return jnp.sum(jnp.where(mask, 1.0, 0.0), axis=axis, keepdims=True)


def exchange_rows(listed_row, rows):
    n = listed_row.shape[1]
    keep = float(rows - n)
    down = lax.broadcasted_iota(jnp.int32, (n, n), 0).astype(jnp.float32)
    along = lax.broadcasted_iota(jnp.int32, (n, n), 1).astype(jnp.float32)
    diagonal = down == along
    listed_col = jnp.sum(
        jnp.where(diagonal, listed_row, 0.0), axis=1, keepdims=True
    )
    used_row = counted(listed_col == along + keep, 0)
    used_col = counted(listed_row == down + keep, 1)
    free_rank = jnp.sum(
        jnp.where(down < along, 1.0 - used_col, 0.0), axis=0, keepdims=True
    )
    low_rank = counted(jnp.logical_and(along < down, listed_row < keep), 1)
    match = jnp.logical_and(low_rank == free_rank, used_row == 0.0)
    found = jnp.sum(jnp.where(match, along + keep, 0.0), axis=1, keepdims=True)
    found = jnp.where(listed_col < keep, found, listed_col)
    found_row = jnp.sum(jnp.where(diagonal, found, 0.0), axis=0, keepdims=True)
    return listed_col, found_row


def pack_kernel(
    lists, fresh, early, bulk, held, mine, plan, where, list_sem, plan_sem, in_sem, out_sem
):
    _, slots, rows, _, _ = fresh.shape
    listed = early.shape[2]
    keep = rows - listed
    step = 8
    group = lax.axis_index("grp")
    load_list = pltpu.make_async_copy(lists.at[group], mine, list_sem)
    load_list.start()
    loads = [
        pltpu.make_async_copy(fresh.at[0, s], held.at[s], in_sem.at[s])
        for s in range(slots)
    ]
    for load in loads:
        load.start()
    load_list.wait()
    for s in range(slots):
        listed_row = mine[s : s + 1, :]
        _, found = exchange_rows(listed_row.astype(jnp.float32), rows)
        plan[2 * s : 2 * s + 1, :listed] = listed_row
        plan[2 * s + 1 : 2 * s + 2, :listed] = found.astype(jnp.int32)
    move = pltpu.make_async_copy(plan, where, plan_sem)
    move.start()
    move.wait()
    stores = []
    for s in range(slots):
        loads[s].wait()

        def exchange(i, carry, s=s):
            ids = [i * step + k for k in range(step)]
            at = [where[2 * s, j] for j in ids]
            to = [where[2 * s + 1, j] for j in ids]
            taken = [held[s, row] for row in at]
            given = [held[s, row] for row in to]
            for k in range(step):
                early[0, s, ids[k]] = taken[k]
            for k in range(step):
                held[s, at[k]] = given[k]
            return carry

        lax.fori_loop(0, listed // step, exchange, 0)
        store = pltpu.make_async_copy(
            held.at[s, pl.ds(0, keep)], bulk.at[0, s], out_sem.at[s]
        )
        store.start()
        stores.append(store)
    for store in stores:
        store.wait()


def pack(refresh_rows, fresh_kv):
    _, slots, rows, two, width = fresh_kv.shape
    listed = refresh_rows.shape[2]
    keep = rows - listed
    kv = fresh_kv.dtype
    return pl.pallas_call(
        pack_kernel,
        out_shape=(
            jax.ShapeDtypeStruct((1, slots, listed, two, width), kv),
            jax.ShapeDtypeStruct((1, slots, keep, two, width), kv),
        ),
        in_specs=[whole(HBM), whole(HBM)],
        out_specs=(whole(VMEM), whole(pl.ANY)),
        scratch_shapes=[
            pltpu.VMEM((slots, rows, two, width), kv),
            pltpu.VMEM((slots, listed), jnp.int32),
            pltpu.VMEM((8, TILE), jnp.int32),
            pltpu.SMEM((8, TILE), jnp.int32),
            pltpu.SemaphoreType.DMA,
            pltpu.SemaphoreType.DMA,
            pltpu.SemaphoreType.DMA((slots,)),
            pltpu.SemaphoreType.DMA((slots,)),
        ],
        compiler_params=pltpu.CompilerParams(vmem_limit_bytes=8 << 20),
        cost_estimate=pl.CostEstimate(
            flops=0, transcendentals=0, bytes_accessed=4 << 20
        ),
        name="pack",
    )(refresh_rows, fresh_kv)


def unpack_kernel(where, early, bulk, out, passed, held, in_sem, out_sem):
    passed[...] = jnp.zeros_like(passed)
    _, slots, rows, _, _ = out.shape
    listed = early.shape[2]
    keep = rows - listed
    step = 8
    loads = [
        pltpu.make_async_copy(
            bulk.at[0, s], held.at[s, pl.ds(0, keep)], in_sem.at[s]
        )
        for s in range(slots)
    ]
    for load in loads:
        load.start()
    stores = []
    for s in range(slots):
        loads[s].wait()

        def place(i, carry, s=s):
            ids = [i * step + k for k in range(step)]
            at = [where[2 * s, j] for j in ids]
            to = [where[2 * s + 1, j] for j in ids]
            moved = [held[s, row] for row in at]
            new = [early[0, s, j] for j in ids]
            for k in range(step):
                held[s, to[k]] = moved[k]
            for k in range(step):
                held[s, at[k]] = new[k]
            return carry

        lax.fori_loop(0, listed // step, place, 0)
        store = pltpu.make_async_copy(held.at[s], out.at[0, s], out_sem.at[s])
        store.start()
        stores.append(store)
    for store in stores:
        store.wait()


def unpack(where, early, bulk):
    _, slots, listed, two, width = early.shape
    rows = bulk.shape[2] + listed
    kv = bulk.dtype
    return pl.pallas_call(
        unpack_kernel,
        out_shape=(
            jax.ShapeDtypeStruct((1, slots, rows, two, width), kv),
            jax.ShapeDtypeStruct((8, TILE), jnp.float32),
        ),
        in_specs=[whole(SMEM), whole(VMEM), whole(pl.ANY)],
        out_specs=(whole(pl.ANY), whole(VMEM)),
        scratch_shapes=[
            pltpu.VMEM((slots, rows, two, width), kv),
            pltpu.SemaphoreType.DMA((slots,)),
            pltpu.SemaphoreType.DMA((slots,)),
        ],
        compiler_params=pltpu.CompilerParams(vmem_limit_bytes=8 << 20),
        cost_estimate=pl.CostEstimate(
            flops=0, transcendentals=0, bytes_accessed=4 << 20
        ),
        name="unpack",
    )(where, early, bulk)


def finish_kernel(kept, other, shown, step_size, latent, after, velocity, latent_next):
    _, slots, _, ch = latent.shape
    total = kept[...] + other[...].astype(jnp.float32)
    for s in range(slots):
        v = jnp.where(shown[s] > 0.0, total[:, s * ch : (s + 1) * ch], 0.0)
        velocity[0, s] = v
        latent_next[0, s] = latent[0, s] + step_size[s] * v


def finish(kept, other, shown, step_size, latent, after):
    return pl.pallas_call(
        finish_kernel,
        out_shape=(jax.ShapeDtypeStruct(latent.shape, jnp.float32),) * 2,
        in_specs=[whole(VMEM)] * 6,
        out_specs=(whole(VMEM),) * 2,
        compiler_params=pltpu.CompilerParams(vmem_limit_bytes=4 << 20),
        cost_estimate=pl.CostEstimate(
            flops=0, transcendentals=0, bytes_accessed=1 << 18
        ),
        name="finish",
    )(kept, other, shown, step_size, latent, after)


def prepare_kernel(
    lists,
    live,
    requests,
    times,
    queries,
    bias,
    where,
    shown,
    step,
    queries_near,
    theirs,
    list_sem,
    q_sem,
):
    load_q = pltpu.make_async_copy(queries, queries_near, q_sem)
    load_q.start()
    slots = bias.shape[0]
    listed = lists.shape[2]
    rows = (bias.shape[2] - TILE) // 2
    groups = lax.axis_size("grp")
    group = lax.axis_index("grp")
    partner = lax.rem(group + groups // 2, groups)
    load_list = pltpu.make_async_copy(lists.at[partner], theirs, list_sem)
    load_list.start()
    ids = lax.broadcasted_iota(jnp.int32, (1, rows), 1)
    ids_down = lax.broadcasted_iota(jnp.int32, (listed, rows), 1).astype(jnp.float32)
    dead = jnp.float32(-jnp.inf)
    load_list.wait()
    for s in range(slots):
        partner_live = live[s, partner]
        listed_row = theirs[s : s + 1, :]
        listed_col, found = exchange_rows(listed_row.astype(jnp.float32), rows)
        where[2 * s : 2 * s + 1, :listed] = listed_row
        where[2 * s + 1 : 2 * s + 2, :listed] = found.astype(jnp.int32)
        replaced = counted(ids_down == listed_col, 0) > 0.0
        counts = jnp.logical_and(ids < partner_live, jnp.logical_not(replaced))
        bias[s, :, :rows] = jnp.where(ids < live[s, group], 0.0, dead)
        bias[s, :, rows : 2 * rows] = jnp.where(counts, 0.0, dead)
        bias[s, :, 2 * rows :] = jnp.full((1, TILE), dead)
        bias[s, :, 2 * rows : 2 * rows + listed] = jnp.where(
            listed_row < partner_live, 0.0, dead
        )
    _, share, ch = shown.shape
    share_ids = lax.axis_index("tp") * share + lax.broadcasted_iota(
        jnp.int32, (share, ch), 0
    )
    pair = lax.rem(group, groups // 2)
    for s in range(slots):
        request = requests[pair * slots + s]
        gap = times[1, request] - times[0, request]
        shown[s] = jnp.where(share_ids < live[s, group], 1.0, 0.0)
        step[s] = jnp.full((share, ch), gap, jnp.int32).astype(jnp.float32) / 1000.0
    load_q.wait()


def prepare(refresh_rows, live_t, request_list, times_t, queries, latent):
    rows = queries.shape[2]
    _, slots, listed = refresh_rows.shape
    aside = jax.ShapeDtypeStruct(latent.shape[1:], jnp.float32)
    return pl.pallas_call(
        prepare_kernel,
        out_shape=(
            jax.ShapeDtypeStruct((slots, 1, 2 * rows + TILE), jnp.float32),
            jax.ShapeDtypeStruct((8, TILE), jnp.int32),
            aside,
            aside,
            jax.ShapeDtypeStruct(queries.shape, queries.dtype),
        ),
        in_specs=[whole(HBM), whole(SMEM), whole(SMEM), whole(SMEM), whole(HBM)],
        out_specs=(whole(VMEM),) * 5,
        scratch_shapes=[
            pltpu.VMEM((slots, listed), jnp.int32),
            pltpu.SemaphoreType.DMA,
            pltpu.SemaphoreType.DMA,
        ],
        compiler_params=pltpu.CompilerParams(vmem_limit_bytes=4 << 20),
        cost_estimate=pl.CostEstimate(
            flops=0, transcendentals=0, bytes_accessed=1 << 20
        ),
        name="prepare",
    )(refresh_rows, live_t, request_list, times_t, queries)


def tiles(array):
    return [array[:, i : i + TILE] for i in range(0, array.shape[1], TILE)]


def attend_kernel(
    bias,
    q,
    own,
    stale,
    text,
    text_other,
    early,
    w_t,
    kept,
    away,
    scores,
    packed,
    leaving,
    arrived,
    send,
    recv,
):
    slot = pl.program_id(0)
    t = lax.axis_index("tp")
    x, half = t // 2, lax.rem(t, 2)
    sides = lax.axis_size("tp") // 2
    share = kept.shape[0]
    peers = [lax.rem(x + d, sides) * 2 + half for d in range(1, sides)]

    def along_x(s, i):
        at = pl.multiple_of(peers[i] // 2 * share, share)
        return pltpu.make_async_remote_copy(
            src_ref=leaving.at[s, pl.ds(at, share)],
            dst_ref=arrived.at[s, i],
            send_sem=send.at[s, i],
            recv_sem=recv.at[s, i],
            device_id={"tp": peers[i]},
            device_id_type=pl.DeviceIdType.MESH,
        )

    barrier = pltpu.get_barrier_semaphore()

    @pl.when(slot == 0)
    def _():
        for peer in peers:
            pl.semaphore_signal(
                barrier,
                inc=1,
                device_id={"tp": peer},
                device_id_type=pl.DeviceIdType.MESH,
            )

    rows = own.shape[2]
    heads = q.shape[3] // HD
    part_rows = scores.shape[1]
    ch = w_t.shape[0]
    blocks = (
        (own, 0, bias[0, :, :rows]),
        (stale, rows, bias[0, :, rows : 2 * rows]),
        (early, 2 * rows, bias[0, :, 2 * rows :]),
        (text, 2 * rows + TILE, None),
        (text_other, 2 * rows + TILE + text.shape[2], None),
    )

    def score(unit, place, block, top):
        head, first = unit
        kv, at, block_bias = block
        s = lax.dot_general(
            q[0, 0, first : first + part_rows, head * HD : (head + 1) * HD],
            kv[0, 0, :, head * HD : (head + 1) * HD],
            (((1,), (1,)), ((), ())),
            preferred_element_type=jnp.float32,
        )
        if block_bias is not None:
            s = s + block_bias
        scores[place, :, at : at + s.shape[1]] = s
        for tile in tiles(s):
            top = tile if top is None else jnp.maximum(top, tile)
        return top

    def weigh(unit, place, block, shift, total, blended):
        head, _ = unit
        kv, at, _ = block
        weights = jnp.exp2(
            scores[place, :, at : at + kv.shape[2]] * SCALE - shift
        )
        for tile in tiles(weights):
            total = tile if total is None else total + tile
        part = jnp.dot(
            weights.astype(jnp.bfloat16),
            kv[0, 1, :, head * HD : (head + 1) * HD],
            preferred_element_type=jnp.float32,
        )
        return total, part if blended is None else blended + part

    units = [
        (head, first)
        for first in range(0, rows, part_rows)
        for head in range(heads)
    ]
    top = None
    for block in blocks:
        top = score(units[0], 0, block, top)
    velocity = {}
    for i, unit in enumerate(units):
        shift = jnp.max(top, axis=1, keepdims=True) * SCALE
        top = total = blended = None
        for block in blocks:
            if i + 1 < len(units):
                top = score(units[i + 1], (i + 1) % 2, block, top)
            total, blended = weigh(unit, i % 2, block, shift, total, blended)
        total = jnp.sum(total, axis=1, keepdims=True)
        head, first = unit
        v = lax.dot_general(
            (blended / total).astype(jnp.bfloat16),
            w_t[:, head * HD : (head + 1) * HD],
            (((1,), (1,)), ((), ())),
            preferred_element_type=jnp.float32,
        )
        velocity[first] = v if first not in velocity else velocity[first] + v

    for first, v in velocity.items():
        for at in range(0, part_rows, 2 * share):
            both = jnp.concatenate(
                [v[at : at + share], v[at + share : at + 2 * share]], axis=1
            )
            to = (first + at) // 2
            packed[slot, to : to + share] = both
            leaving[slot, to : to + share] = both.astype(leaving.dtype)

    @pl.when(slot == 0)
    def _():
        pl.semaphore_wait(barrier, sides - 1)

    for i in range(sides - 1):
        along_x(slot, i).start()

    @pl.when(slot == pl.num_programs(0) - 1)
    def _():
        for s in range(arrived.shape[0]):
            total = packed[s, pl.ds(pl.multiple_of(x * share, share), share)]
            for i in range(sides - 1):
                along_x(s, i).wait_recv()
                total = total + arrived[s, i].astype(jnp.float32)
            low, high = total[:, :ch], total[:, ch:]
            lanes = slice(s * ch, (s + 1) * ch)
            kept[:, lanes] = jnp.where(half == 0, low, high)
            away[:, lanes] = jnp.where(half == 0, high, low).astype(away.dtype)
        for s in range(arrived.shape[0]):
            for i in range(sides - 1):
                along_x(s, i).wait_send()


def attend(bias, queries, own, stale, text, text_other, early, w_t, members):
    _, slots, rows, inner = queries.shape
    ch = w_t.shape[0]
    keys = sum(a.shape[2] for a in (own, stale, text, text_other, early))
    share, sides = rows // members, members // 2
    sent = jnp.bfloat16

    def kv_spec(a):
        return pl.BlockSpec((1, 2, a.shape[2], inner), lambda s: (s, 0, 0, 0))

    return pl.pallas_call(
        attend_kernel,
        grid=(slots,),
        out_shape=(
            jax.ShapeDtypeStruct((share, slots * ch), jnp.float32),
            jax.ShapeDtypeStruct((share, slots * ch), sent),
        ),
        in_specs=[
            pl.BlockSpec((1, 1, bias.shape[2]), lambda s: (s, 0, 0)),
            pl.BlockSpec((1, 1, rows, inner), lambda s: (0, s, 0, 0)),
            kv_spec(own),
            kv_spec(stale),
            kv_spec(text),
            kv_spec(text_other),
            kv_spec(early),
            pl.BlockSpec((ch, inner), lambda s: (0, 0)),
        ],
        out_specs=(pl.BlockSpec((share, slots * ch), lambda s: (0, 0)),) * 2,
        scratch_shapes=[
            pltpu.VMEM((2, rows // 2, keys), jnp.float32),
            pltpu.VMEM((slots, rows // 2, 2 * ch), jnp.float32),
            pltpu.VMEM((slots, rows // 2, 2 * ch), sent),
            pltpu.VMEM((slots, sides - 1, share, 2 * ch), sent),
            pltpu.SemaphoreType.DMA((slots, sides - 1)),
            pltpu.SemaphoreType.DMA((slots, sides - 1)),
        ],
        compiler_params=pltpu.CompilerParams(
            collective_id=0, has_side_effects=True, vmem_limit_bytes=24 << 20
        ),
        cost_estimate=pl.CostEstimate(
            flops=40 * slots * rows * keys * inner,
            transcendentals=slots * rows * keys * inner // HD,
            bytes_accessed=4 << 20,
        ),
        name="attend",
    )(bias, queries, own, stale, text, text_other, early, w_t)


def in_order(array):
    return with_layout_constraint(array, Layout(tuple(range(array.ndim))))


def apart(kv):
    return jnp.transpose(kv[0], (0, 2, 1, 3))


def shards(
    queries,
    fresh_kv,
    stale_kv,
    text_kv,
    w_velocity,
    latent,
    live_counts,
    refresh_rows,
    request_list,
    timesteps,
):
    half_groups = lax.axis_size("grp") // 2
    live_t = live_counts.T
    times_t = timesteps.T
    listed = refresh_rows.shape[2]
    text_other = in_order(from_behind(in_order(text_kv), "grp", half_groups))
    early_out, bulk_out = pack(refresh_rows, fresh_kv)
    early = in_order(from_behind(in_order(early_out), "grp", half_groups))
    bias, where, shown, step_size, near = prepare(
        refresh_rows, live_t, request_list, times_t, queries, latent
    )
    own, stale, text = apart(fresh_kv), apart(stale_kv), apart(text_kv)
    bulk_out, bias, where, near, own, stale, text = lax.optimization_barrier(
        (bulk_out, bias, where, near, own, stale, text)
    )
    bulk = from_behind(bulk_out, "grp", half_groups)
    early_apart = jnp.pad(apart(early), ((0, 0), (0, 0), (0, TILE - listed), (0, 0)))
    kept, away = attend(
        bias,
        near,
        own,
        stale,
        text,
        apart(text_other),
        early_apart,
        w_velocity.T,
        lax.axis_size("tp"),
    )
    members = range(lax.axis_size("tp"))
    other = lax.ppermute(away, "tp", [(i, i ^ 1) for i in members])
    next_stale, passed = unpack(where, early, bulk)
    velocity, latent_next = finish(
        kept, other, shown, step_size, latent, passed
    )
    return next_stale, velocity, latent_next


def solution(mesh):
    return jax.shard_map(
        shards,
        mesh=mesh,
        in_specs=(
            P("grp", None, None, "tp"),
            P("grp", None, None, None, "tp"),
            P("grp", None, None, None, "tp"),
            P("grp", None, None, None, "tp"),
            P("tp", None),
            P("grp", None, "tp", None),
            P(),
            P(),
            P(),
            P(),
        ),
        out_specs=(
            P("grp", None, None, None, "tp"),
            P("grp", None, "tp", None),
            P("grp", None, "tp", None),
        ),
        check_vma=False,
    )
```

```python
import math

import jax
import jax.numpy as jnp
from jax import lax
from jax.experimental.layout import Layout, with_layout_constraint
from jax.experimental import pallas as pl
from jax.experimental.pallas import tpu as pltpu
from jax.sharding import PartitionSpec as P

HD = 128
TILE = 128
SCALE = math.log2(math.e) / math.sqrt(HD)
VMEM = pltpu.MemorySpace.VMEM
SMEM = pltpu.MemorySpace.SMEM
HBM = pltpu.MemorySpace.HBM


def whole(space):
    return pl.BlockSpec(memory_space=space)


def from_behind(block, axis, distance):
    devices = range(lax.axis_size(axis))
    route = [((i - distance) % len(devices), i) for i in devices]
    return lax.ppermute(block, axis, route)


def counted(mask, axis):
    return jnp.sum(jnp.where(mask, 1.0, 0.0), axis=axis, keepdims=True)


def exchange_rows(listed_row, rows):
    n = listed_row.shape[1]
    keep = float(rows - n)
    down = lax.broadcasted_iota(jnp.int32, (n, n), 0).astype(jnp.float32)
    along = lax.broadcasted_iota(jnp.int32, (n, n), 1).astype(jnp.float32)
    diagonal = down == along
    listed_col = jnp.sum(
        jnp.where(diagonal, listed_row, 0.0), axis=1, keepdims=True
    )
    used_row = counted(listed_col == along + keep, 0)
    used_col = counted(listed_row == down + keep, 1)
    free_rank = jnp.sum(
        jnp.where(down < along, 1.0 - used_col, 0.0), axis=0, keepdims=True
    )
    low_rank = counted(jnp.logical_and(along < down, listed_row < keep), 1)
    match = jnp.logical_and(low_rank == free_rank, used_row == 0.0)
    found = jnp.sum(jnp.where(match, along + keep, 0.0), axis=1, keepdims=True)
    found = jnp.where(listed_col < keep, found, listed_col)
    found_row = jnp.sum(jnp.where(diagonal, found, 0.0), axis=0, keepdims=True)
    return listed_col, found_row


def pack_kernel(
    lists, fresh, early, bulk, held, mine, plan, where, list_sem, plan_sem, in_sem, out_sem
):
    _, slots, rows, _, _ = fresh.shape
    listed = early.shape[2]
    keep = rows - listed
    step = 8
    group = lax.axis_index("grp")
    load_list = pltpu.make_async_copy(lists.at[group], mine, list_sem)
    load_list.start()
    loads = [
        pltpu.make_async_copy(fresh.at[0, s], held.at[s], in_sem.at[s])
        for s in range(slots)
    ]
    for load in loads:
        load.start()
    load_list.wait()
    for s in range(slots):
        listed_row = mine[s : s + 1, :]
        _, found = exchange_rows(listed_row.astype(jnp.float32), rows)
        plan[2 * s : 2 * s + 1, :listed] = listed_row
        plan[2 * s + 1 : 2 * s + 2, :listed] = found.astype(jnp.int32)
    move = pltpu.make_async_copy(plan, where, plan_sem)
    move.start()
    move.wait()
    stores = []
    for s in range(slots):
        loads[s].wait()

        def exchange(i, carry, s=s):
            ids = [i * step + k for k in range(step)]
            at = [where[2 * s, j] for j in ids]
            to = [where[2 * s + 1, j] for j in ids]
            taken = [held[s, row] for row in at]
            given = [held[s, row] for row in to]
            for k in range(step):
                early[0, s, ids[k]] = taken[k]
            for k in range(step):
                held[s, at[k]] = given[k]
            return carry

        lax.fori_loop(0, listed // step, exchange, 0)
        store = pltpu.make_async_copy(
            held.at[s, pl.ds(0, keep)], bulk.at[0, s], out_sem.at[s]
        )
        store.start()
        stores.append(store)
    for store in stores:
        store.wait()


def pack(refresh_rows, fresh_kv):
    _, slots, rows, two, width = fresh_kv.shape
    listed = refresh_rows.shape[2]
    keep = rows - listed
    kv = fresh_kv.dtype
    return pl.pallas_call(
        pack_kernel,
        out_shape=(
            jax.ShapeDtypeStruct((1, slots, listed, two, width), kv),
            jax.ShapeDtypeStruct((1, slots, keep, two, width), kv),
        ),
        in_specs=[whole(HBM), whole(HBM)],
        out_specs=(whole(VMEM), whole(pl.ANY)),
        scratch_shapes=[
            pltpu.VMEM((slots, rows, two, width), kv),
            pltpu.VMEM((slots, listed), jnp.int32),
            pltpu.VMEM((8, TILE), jnp.int32),
            pltpu.SMEM((8, TILE), jnp.int32),
            pltpu.SemaphoreType.DMA,
            pltpu.SemaphoreType.DMA,
            pltpu.SemaphoreType.DMA((slots,)),
            pltpu.SemaphoreType.DMA((slots,)),
        ],
        compiler_params=pltpu.CompilerParams(vmem_limit_bytes=8 << 20),
        cost_estimate=pl.CostEstimate(
            flops=0, transcendentals=0, bytes_accessed=4 << 20
        ),
        name="pack",
    )(refresh_rows, fresh_kv)


def unpack_kernel(
    plan, early, bulk, out, passed, held, where, plan_sem, in_sem, out_sem
):
    move = pltpu.make_async_copy(plan, where, plan_sem)
    move.start()
    _, slots, rows, _, _ = out.shape
    listed = early.shape[2]
    keep = rows - listed
    step = 8
    loads = [
        pltpu.make_async_copy(
            bulk.at[0, s], held.at[s, pl.ds(0, keep)], in_sem.at[s]
        )
        for s in range(slots)
    ]
    for load in loads:
        load.start()
    passed[...] = jnp.zeros_like(passed)
    move.wait()
    stores = []
    for s in range(slots):
        loads[s].wait()

        def place(i, carry, s=s):
            ids = [i * step + k for k in range(step)]
            at = [where[2 * s, j] for j in ids]
            to = [where[2 * s + 1, j] for j in ids]
            moved = [held[s, row] for row in at]
            new = [early[0, s, j] for j in ids]
            for k in range(step):
                held[s, to[k]] = moved[k]
            for k in range(step):
                held[s, at[k]] = new[k]
            return carry

        lax.fori_loop(0, listed // step, place, 0)
        store = pltpu.make_async_copy(held.at[s], out.at[0, s], out_sem.at[s])
        store.start()
        stores.append(store)
    for store in stores:
        store.wait()


def unpack(where, early, bulk):
    _, slots, listed, two, width = early.shape
    rows = bulk.shape[2] + listed
    kv = bulk.dtype
    return pl.pallas_call(
        unpack_kernel,
        out_shape=(
            jax.ShapeDtypeStruct((1, slots, rows, two, width), kv),
            jax.ShapeDtypeStruct((8, TILE), jnp.float32),
        ),
        in_specs=[whole(VMEM), whole(VMEM), whole(pl.ANY)],
        out_specs=(whole(pl.ANY), whole(VMEM)),
        scratch_shapes=[
            pltpu.VMEM((slots, rows, two, width), kv),
            pltpu.SMEM(where.shape, where.dtype),
            pltpu.SemaphoreType.DMA,
            pltpu.SemaphoreType.DMA((slots,)),
            pltpu.SemaphoreType.DMA((slots,)),
        ],
        compiler_params=pltpu.CompilerParams(vmem_limit_bytes=8 << 20),
        cost_estimate=pl.CostEstimate(
            flops=0, transcendentals=0, bytes_accessed=4 << 20
        ),
        name="unpack",
    )(where, early, bulk)


def finish_kernel(kept, other, shown, step_size, latent, after, velocity, latent_next):
    _, slots, _, ch = latent.shape
    total = kept[...] + other[...].astype(jnp.float32)
    for s in range(slots):
        v = jnp.where(shown[s] > 0.0, total[:, s * ch : (s + 1) * ch], 0.0)
        velocity[0, s] = v
        latent_next[0, s] = latent[0, s] + step_size[s] * v


def finish(kept, other, shown, step_size, latent, after):
    return pl.pallas_call(
        finish_kernel,
        out_shape=(jax.ShapeDtypeStruct(latent.shape, jnp.float32),) * 2,
        in_specs=[whole(VMEM)] * 6,
        out_specs=(whole(VMEM),) * 2,
        compiler_params=pltpu.CompilerParams(vmem_limit_bytes=4 << 20),
        cost_estimate=pl.CostEstimate(
            flops=0, transcendentals=0, bytes_accessed=1 << 18
        ),
        name="finish",
    )(kept, other, shown, step_size, latent, after)


def prepare_kernel(
    lists,
    live,
    requests,
    times,
    queries,
    bias,
    where,
    shown,
    step,
    queries_near,
    theirs,
    list_sem,
    q_sem,
):
    load_q = pltpu.make_async_copy(queries, queries_near, q_sem)
    load_q.start()
    slots = bias.shape[0]
    listed = lists.shape[2]
    rows = (bias.shape[2] - TILE) // 2
    groups = lax.axis_size("grp")
    group = lax.axis_index("grp")
    partner = lax.rem(group + groups // 2, groups)
    load_list = pltpu.make_async_copy(lists.at[partner], theirs, list_sem)
    load_list.start()
    ids = lax.broadcasted_iota(jnp.int32, (1, rows), 1)
    ids_down = lax.broadcasted_iota(jnp.int32, (listed, rows), 1).astype(jnp.float32)
    dead = jnp.float32(-jnp.inf)
    load_list.wait()
    for s in range(slots):
        partner_live = live[s, partner]
        listed_row = theirs[s : s + 1, :]
        listed_col, found = exchange_rows(listed_row.astype(jnp.float32), rows)
        where[2 * s : 2 * s + 1, :listed] = listed_row
        where[2 * s + 1 : 2 * s + 2, :listed] = found.astype(jnp.int32)
        replaced = counted(ids_down == listed_col, 0) > 0.0
        counts = jnp.logical_and(ids < partner_live, jnp.logical_not(replaced))
        bias[s, :, :rows] = jnp.where(ids < live[s, group], 0.0, dead)
        bias[s, :, rows : 2 * rows] = jnp.where(counts, 0.0, dead)
        bias[s, :, 2 * rows :] = jnp.full((1, TILE), dead)
        bias[s, :, 2 * rows : 2 * rows + listed] = jnp.where(
            listed_row < partner_live, 0.0, dead
        )
    _, share, ch = shown.shape
    share_ids = lax.axis_index("tp") * share + lax.broadcasted_iota(
        jnp.int32, (share, ch), 0
    )
    pair = lax.rem(group, groups // 2)
    for s in range(slots):
        request = requests[pair * slots + s]
        gap = times[1, request] - times[0, request]
        shown[s] = jnp.where(share_ids < live[s, group], 1.0, 0.0)
        step[s] = jnp.full((share, ch), gap, jnp.int32).astype(jnp.float32) / 1000.0
    load_q.wait()


def prepare(refresh_rows, live_t, request_list, times_t, queries, latent):
    rows = queries.shape[2]
    _, slots, listed = refresh_rows.shape
    aside = jax.ShapeDtypeStruct(latent.shape[1:], jnp.float32)
    return pl.pallas_call(
        prepare_kernel,
        out_shape=(
            jax.ShapeDtypeStruct((slots, 1, 2 * rows + TILE), jnp.float32),
            jax.ShapeDtypeStruct((8, TILE), jnp.int32),
            aside,
            aside,
            jax.ShapeDtypeStruct(queries.shape, queries.dtype),
        ),
        in_specs=[whole(HBM), whole(SMEM), whole(SMEM), whole(SMEM), whole(HBM)],
        out_specs=(whole(VMEM),) * 5,
        scratch_shapes=[
            pltpu.VMEM((slots, listed), jnp.int32),
            pltpu.SemaphoreType.DMA,
            pltpu.SemaphoreType.DMA,
        ],
        compiler_params=pltpu.CompilerParams(vmem_limit_bytes=4 << 20),
        cost_estimate=pl.CostEstimate(
            flops=0, transcendentals=0, bytes_accessed=1 << 20
        ),
        name="prepare",
    )(refresh_rows, live_t, request_list, times_t, queries)


def tiles(array):
    return [array[:, i : i + TILE] for i in range(0, array.shape[1], TILE)]


def attend_kernel(
    bias,
    q,
    own,
    stale,
    text,
    text_other,
    early,
    w_t,
    kept,
    away,
    scores,
    packed,
    leaving,
    arrived,
    send,
    recv,
):
    slot = pl.program_id(0)
    t = lax.axis_index("tp")
    x, half = t // 2, lax.rem(t, 2)
    sides = lax.axis_size("tp") // 2
    share = kept.shape[0]
    peers = [lax.rem(x + d, sides) * 2 + half for d in range(1, sides)]

    def along_x(s, i):
        at = pl.multiple_of(peers[i] // 2 * share, share)
        return pltpu.make_async_remote_copy(
            src_ref=leaving.at[s, pl.ds(at, share)],
            dst_ref=arrived.at[s, i],
            send_sem=send.at[s, i],
            recv_sem=recv.at[s, i],
            device_id={"tp": peers[i]},
            device_id_type=pl.DeviceIdType.MESH,
        )

    barrier = pltpu.get_barrier_semaphore()

    @pl.when(slot == 0)
    def _():
        for peer in peers:
            pl.semaphore_signal(
                barrier,
                inc=1,
                device_id={"tp": peer},
                device_id_type=pl.DeviceIdType.MESH,
            )

    rows = own.shape[2]
    heads = q.shape[3] // HD
    part_rows = scores.shape[1]
    ch = w_t.shape[0]
    blocks = (
        (own, 0, bias[0, :, :rows]),
        (stale, rows, bias[0, :, rows : 2 * rows]),
        (early, 2 * rows, bias[0, :, 2 * rows :]),
        (text, 2 * rows + TILE, None),
        (text_other, 2 * rows + TILE + text.shape[2], None),
    )

    def score(unit, place, block, top):
        head, first = unit
        kv, at, block_bias = block
        s = lax.dot_general(
            q[0, 0, first : first + part_rows, head * HD : (head + 1) * HD],
            kv[0, 0, :, head * HD : (head + 1) * HD],
            (((1,), (1,)), ((), ())),
            preferred_element_type=jnp.float32,
        )
        if block_bias is not None:
            s = s + block_bias
        scores[place, :, at : at + s.shape[1]] = s
        for tile in tiles(s):
            top = tile if top is None else jnp.maximum(top, tile)
        return top

    def weigh(unit, place, block, shift, total, blended):
        head, _ = unit
        kv, at, _ = block
        weights = jnp.exp2(
            scores[place, :, at : at + kv.shape[2]] * SCALE - shift
        )
        for tile in tiles(weights):
            total = tile if total is None else total + tile
        part = jnp.dot(
            weights.astype(jnp.bfloat16),
            kv[0, 1, :, head * HD : (head + 1) * HD],
            preferred_element_type=jnp.float32,
        )
        return total, part if blended is None else blended + part

    units = [
        (head, first)
        for first in range(0, rows, part_rows)
        for head in range(heads)
    ]
    top = None
    for block in blocks:
        top = score(units[0], 0, block, top)
    velocity = {}
    for i, unit in enumerate(units):
        shift = jnp.max(top, axis=1, keepdims=True) * SCALE
        top = total = blended = None
        for block in blocks:
            if i + 1 < len(units):
                top = score(units[i + 1], (i + 1) % 2, block, top)
            total, blended = weigh(unit, i % 2, block, shift, total, blended)
        total = jnp.sum(total, axis=1, keepdims=True)
        head, first = unit
        v = lax.dot_general(
            (blended / total).astype(jnp.bfloat16),
            w_t[:, head * HD : (head + 1) * HD],
            (((1,), (1,)), ((), ())),
            preferred_element_type=jnp.float32,
        )
        velocity[first] = v if first not in velocity else velocity[first] + v

    for first, v in velocity.items():
        for at in range(0, part_rows, 2 * share):
            both = jnp.concatenate(
                [v[at : at + share], v[at + share : at + 2 * share]], axis=1
            )
            to = (first + at) // 2
            packed[slot, to : to + share] = both
            leaving[slot, to : to + share] = both.astype(leaving.dtype)

    @pl.when(slot == 0)
    def _():
        pl.semaphore_wait(barrier, sides - 1)

    for i in range(sides - 1):
        along_x(slot, i).start()

    @pl.when(slot == pl.num_programs(0) - 1)
    def _():
        for s in range(arrived.shape[0]):
            total = packed[s, pl.ds(pl.multiple_of(x * share, share), share)]
            for i in range(sides - 1):
                along_x(s, i).wait_recv()
                total = total + arrived[s, i].astype(jnp.float32)
            low, high = total[:, :ch], total[:, ch:]
            lanes = slice(s * ch, (s + 1) * ch)
            kept[:, lanes] = jnp.where(half == 0, low, high)
            away[:, lanes] = jnp.where(half == 0, high, low).astype(away.dtype)
        for s in range(arrived.shape[0]):
            for i in range(sides - 1):
                along_x(s, i).wait_send()


def attend(bias, queries, own, stale, text, text_other, early, w_t, members):
    _, slots, rows, inner = queries.shape
    ch = w_t.shape[0]
    keys = sum(a.shape[2] for a in (own, stale, text, text_other, early))
    share, sides = rows // members, members // 2
    sent = jnp.bfloat16

    def kv_spec(a):
        return pl.BlockSpec((1, 2, a.shape[2], inner), lambda s: (s, 0, 0, 0))

    return pl.pallas_call(
        attend_kernel,
        grid=(slots,),
        out_shape=(
            jax.ShapeDtypeStruct((share, slots * ch), jnp.float32),
            jax.ShapeDtypeStruct((share, slots * ch), sent),
        ),
        in_specs=[
            pl.BlockSpec((1, 1, bias.shape[2]), lambda s: (s, 0, 0)),
            pl.BlockSpec((1, 1, rows, inner), lambda s: (0, s, 0, 0)),
            kv_spec(own),
            kv_spec(stale),
            kv_spec(text),
            kv_spec(text_other),
            kv_spec(early),
            pl.BlockSpec((ch, inner), lambda s: (0, 0)),
        ],
        out_specs=(pl.BlockSpec((share, slots * ch), lambda s: (0, 0)),) * 2,
        scratch_shapes=[
            pltpu.VMEM((2, rows // 2, keys), jnp.float32),
            pltpu.VMEM((slots, rows // 2, 2 * ch), jnp.float32),
            pltpu.VMEM((slots, rows // 2, 2 * ch), sent),
            pltpu.VMEM((slots, sides - 1, share, 2 * ch), sent),
            pltpu.SemaphoreType.DMA((slots, sides - 1)),
            pltpu.SemaphoreType.DMA((slots, sides - 1)),
        ],
        compiler_params=pltpu.CompilerParams(
            collective_id=0, has_side_effects=True, vmem_limit_bytes=24 << 20
        ),
        cost_estimate=pl.CostEstimate(
            flops=40 * slots * rows * keys * inner,
            transcendentals=slots * rows * keys * inner // HD,
            bytes_accessed=4 << 20,
        ),
        name="attend",
    )(bias, queries, own, stale, text, text_other, early, w_t)


def in_order(array):
    return with_layout_constraint(array, Layout(tuple(range(array.ndim))))


def apart(kv):
    return jnp.transpose(kv[0], (0, 2, 1, 3))


def shards(
    queries,
    fresh_kv,
    stale_kv,
    text_kv,
    w_velocity,
    latent,
    live_counts,
    refresh_rows,
    request_list,
    timesteps,
):
    half_groups = lax.axis_size("grp") // 2
    live_t = live_counts.T
    times_t = timesteps.T
    listed = refresh_rows.shape[2]
    text_other = in_order(from_behind(in_order(text_kv), "grp", half_groups))
    early_out, bulk_out = pack(refresh_rows, fresh_kv)
    early = in_order(from_behind(in_order(early_out), "grp", half_groups))
    bias, where, shown, step_size, near = prepare(
        refresh_rows, live_t, request_list, times_t, queries, latent
    )
    own, stale, text = apart(fresh_kv), apart(stale_kv), apart(text_kv)
    bulk_out, bias, where, near, own, stale, text = lax.optimization_barrier(
        (bulk_out, bias, where, near, own, stale, text)
    )
    bulk = from_behind(bulk_out, "grp", half_groups)
    early_apart = jnp.pad(apart(early), ((0, 0), (0, 0), (0, TILE - listed), (0, 0)))
    kept, away = attend(
        bias,
        near,
        own,
        stale,
        text,
        apart(text_other),
        early_apart,
        w_velocity.T,
        lax.axis_size("tp"),
    )
    members = range(lax.axis_size("tp"))
    other = lax.ppermute(away, "tp", [(i, i ^ 1) for i in members])
    next_stale, passed = unpack(where, early, bulk)
    velocity, latent_next = finish(
        kept, other, shown, step_size, latent, passed
    )
    return next_stale, velocity, latent_next


def solution(mesh):
    return jax.shard_map(
        shards,
        mesh=mesh,
        in_specs=(
            P("grp", None, None, "tp"),
            P("grp", None, None, None, "tp"),
            P("grp", None, None, None, "tp"),
            P("grp", None, None, None, "tp"),
            P("tp", None),
            P("grp", None, "tp", None),
            P(),
            P(),
            P(),
            P(),
        ),
        out_specs=(
            P("grp", None, None, None, "tp"),
            P("grp", None, "tp", None),
            P("grp", None, "tp", None),
        ),
        check_vma=False,
    )
```
